256 devices in a mesh: depth: 4 (over z_hi), tile: 64 (over x, y, z_lo, core).
Axes of the slice: x: 4, y: 4, z: 8 (z_hi: 4, z_lo: 2; z = z_hi * 2 + z_lo), core: 2. Of those that a mesh axis runs over, the one named last changes fastest.
Arguments:
- amplitude: float32 [8, 64, 256, 256], P('depth', 'tile'), may hold values from 0.7 to 1.3
- phase_map: float32 [8, 64, 256, 256], P('depth', 'tile'), may hold values from -3.140625 to 3.140625
- probe_wave: float32 [2, 128, 128], replicated, may hold values from -4 to 4
- propagator_phase: float32 [2, 128], replicated, may hold values from -3.140625 to 3.140625
- positions: int32 [64, 4, 2], P('tile'), may hold values from -64 to 192
- measured: float32 [64, 4, 128, 128], P('tile'), may hold values from 0 to 1
Outputs:
- object_gradient: float32 [2, 8, 64, 256, 256], P(None, 'depth', 'tile')
The draws below stay inside these ranges and needn't reach their ends.
Inputs may be any that keep to these rules, and one draw needn't show every extreme that they name: `positions`: every window of 128 x 128 pixels starting at a position lies within 64 pixels of its tile.
All inputs are finite; a program needn't handle non-finite values.
Results may differ from the reference program's by a relative error of at most 0.02.
Values may be sent and summed in bfloat16 or wider, within the bound.
No kernel may reach another device: no remote copies, remote signals or barrier semaphores. Data moves between devices by JAX's collectives and lax.ppermute only.
A program may use at most 128 MiB of HBM per device.

```python
import math
import jax
import jax.numpy as jnp
from jax import lax

PROBE = 128
RIM = 64
SLICE_DEV = 2
TILE = 256
WAVES = 4
SLICES = 8
TILES = 64
TCOLS = 8


def plant(values, key, least, high):
    spot = [jax.random.randint(jax.random.fold_in(key, axis), (), 0, length) for axis, length in enumerate(values.shape)]
    main_axis = values.shape.index(max(values.shape))
    next_to = spot[:main_axis] + [(spot[main_axis] + 1) % values.shape[main_axis]] + spot[main_axis + 1:]
    return values.at[tuple(spot)].set(least).at[tuple(next_to)].set(high)


def block_scale(rng, extent, cuts, smallest, largest):
    loudness, own = 1.0, jax.random.fold_in(rng, 6)
    for axis_at, blocks in cuts:
        draws = jnp.exp(jax.random.uniform(jax.random.fold_in(own, axis_at), (blocks,), jnp.float32, smallest / len(cuts), largest / len(cuts)))
        loudness = loudness * jnp.repeat(draws, extent[axis_at] // blocks).reshape([-1 if axis == axis_at else 1 for axis in range(len(extent))])
    return loudness


def scatter_about(own_key, shape, scale, reach, held_as=jnp.bfloat16):
    return jnp.clip(scale * jax.random.normal(own_key, shape, jnp.float32), -reach, reach).astype(held_as)


def setup_inputs(seed: int = 0) -> dict:
    keys = jax.random.split(jax.random.key(seed), 7)
    amplitude = jnp.clip(jnp.exp(math.log(1.3) - 0.6190392 * jax.random.uniform(keys[0], (SLICES, TILES, TILE, TILE), jnp.float32) ** block_scale(keys[0], (SLICES, TILES, TILE, TILE), ((0, 4), (1, 64)), -0.2, 0.2)), 0.7, 1.3)
    phase_map = jnp.clip(jax.random.uniform(keys[1], (SLICES, TILES, TILE, TILE), jnp.float32, -3.140625, 3.140625), -3.140625, 3.140625)
    probe_wave = scatter_about(keys[2], (2, PROBE, PROBE), 0.5, 4.0, jnp.float32)
    propagator_phase = jnp.clip(jax.random.uniform(keys[3], (2, PROBE), jnp.float32, -3.140625, 3.140625), -3.140625, 3.140625)
    positions = plant(jax.random.randint(keys[4], (TILES, WAVES, 2), -RIM, TILE + RIM - PROBE + 1), jax.random.fold_in(keys[4], 1), -RIM, TILE + RIM - PROBE).astype(jnp.int32)
    measured = jnp.clip(1.0 * jax.random.uniform(keys[5], (TILES, WAVES, PROBE, PROBE), jnp.float32) ** block_scale(keys[5], (TILES, WAVES, PROBE, PROBE), ((0, 64),), -0.2, 0.2), 0.0, 1.0)
    return dict(amplitude=amplitude, phase_map=phase_map, probe_wave=probe_wave, propagator_phase=propagator_phase, positions=positions, measured=measured)


PRECISE = lax.Precision.HIGHEST

def dft_tables(points):
    points_line = jnp.arange(points, dtype=jnp.int32)
    products = points_line[:, None] * points_line[None, :] % points
    angles = products.astype(jnp.float32) * (-2.0 * math.pi / points)
    norm_factor = 1.0 / math.sqrt(points)
    return (jnp.cos(angles) * norm_factor, jnp.sin(angles) * norm_factor)

def left_product(mat_real, mat_imag, wave_real, wave_imag):

    def multiply(matrix, operand):
        return jnp.einsum('ij,...jk->...ik', matrix, operand, precision=PRECISE)
    return (multiply(mat_real, wave_real) - multiply(mat_imag, wave_imag), multiply(mat_real, wave_imag) + multiply(mat_imag, wave_real))

def right_product(wave_real, wave_imag, mat_real, mat_imag):

    def multiply(operand, matrix):
        return jnp.einsum('...ij,jk->...ik', operand, matrix, precision=PRECISE)
    return (multiply(wave_real, mat_real) - multiply(wave_imag, mat_imag), multiply(wave_imag, mat_real) + multiply(wave_real, mat_imag))

def build_operators(propagator_phase, tables):
    dft_real, dft_imag = tables
    result = []
    for axis_row in range(2):
        cosine = jnp.cos(propagator_phase[axis_row])[:, None]
        sine_part = jnp.sin(propagator_phase[axis_row])[:, None]
        scaled_real = cosine * dft_real - sine_part * dft_imag
        scaled_imag = cosine * dft_imag + sine_part * dft_real
        result.extend(left_product(dft_real, -dft_imag, scaled_real, scaled_imag))
    return tuple(result)

def to_wire(values):
    return lax.optimization_barrier(values.astype(jnp.bfloat16)).astype(jnp.float32)

def forward_pass(waves, patch_real, patch_imag, operators, group_size):
    row_real, row_imag, col_real, col_imag = operators
    wave_real, wave_imag = (waves[0], waves[1])
    slice_count = patch_real.shape[1]
    kept_real, kept_imag = ([], [])
    for layer_number in range(slice_count):
        kept_real.append(wave_real)
        kept_imag.append(wave_imag)
        slab_real = patch_real[:, layer_number]
        slab_imag = patch_imag[:, layer_number]
        mixed_real = slab_real * wave_real - slab_imag * wave_imag
        mixed_imag = slab_real * wave_imag + slab_imag * wave_real
        half_real, half_imag = left_product(row_real, row_imag, mixed_real, mixed_imag)
        wave_real, wave_imag = right_product(half_real, half_imag, col_real.T, col_imag.T)
        if (layer_number + 1) % group_size == 0 and layer_number + 1 < slice_count:
            wave_real = to_wire(wave_real)
            wave_imag = to_wire(wave_imag)
    return (jnp.stack([wave_real, wave_imag]), jnp.stack(kept_real, axis=1), jnp.stack(kept_imag, axis=1))

def adjoint_pass(backflow, kept_real, kept_imag, patch_real, patch_imag, operators, group_size):
    row_real, row_imag, col_real, col_imag = operators
    back_real, back_imag = (backflow[0], backflow[1])
    slice_count = patch_real.shape[1]
    grads_real = [None] * slice_count
    grads_imag = [None] * slice_count
    for layer_number in reversed(range(slice_count)):
        half_real, half_imag = left_product(row_real.T, -row_imag.T, back_real, back_imag)
        spread_real, spread_imag = right_product(half_real, half_imag, col_real, -col_imag)
        input_real = kept_real[:, layer_number]
        input_imag = kept_imag[:, layer_number]
        grads_real[layer_number] = input_real * spread_real + input_imag * spread_imag
        grads_imag[layer_number] = input_real * spread_imag - input_imag * spread_real
        slab_real = patch_real[:, layer_number]
        slab_imag = patch_imag[:, layer_number]
        back_real = slab_real * spread_real + slab_imag * spread_imag
        back_imag = slab_real * spread_imag - slab_imag * spread_real
        if layer_number % group_size == 0 and layer_number > 0:
            back_real = to_wire(back_real)
            back_imag = to_wire(back_imag)
    return (jnp.stack([back_real, back_imag]), jnp.stack(grads_real, axis=1), jnp.stack(grads_imag, axis=1))

def farfield_residual(waves, observed, tables):
    dft_real, dft_imag = tables
    half_real, half_imag = left_product(dft_real, dft_imag, waves[0], waves[1])
    far_real, far_imag = right_product(half_real, half_imag, dft_real, dft_imag)
    misfit = far_real * far_real + far_imag * far_imag - observed
    inverse_real, inverse_imag = left_product(dft_real, -dft_imag, misfit * far_real, misfit * far_imag)
    back_real, back_imag = right_product(inverse_real, inverse_imag, dft_real, -dft_imag)
    return jnp.stack([back_real, back_imag])

def cut_patches(transmission, windows, points):

    def one_window(window):
        anchor = (jnp.int32(0), jnp.int32(0), window[0], window[1])
        return lax.dynamic_slice(transmission, anchor, (2, transmission.shape[1], points, points))
    patches = jax.vmap(one_window)(windows)
    return (patches[:, 0], patches[:, 1])

def deposit(buffer, grad_real, grad_imag, windows):
    points = grad_real.shape[-1]

    def add_one(number, current):
        window = windows[number]
        anchor = (jnp.int32(0), jnp.int32(0), window[0], window[1])
        previous = lax.dynamic_slice(current, anchor, (2, current.shape[1], points, points))
        fresh = previous + jnp.stack([grad_real[number], grad_imag[number]])
        return lax.dynamic_update_slice(current, fresh, anchor)
    return lax.fori_loop(0, windows.shape[0], add_one, buffer)

def reference(amplitude, phase_map, probe_wave, propagator_phase, positions, measured):
    slice_count = amplitude.shape[0]
    tile_count = amplitude.shape[1]
    tile_size = amplitude.shape[-1]
    grid_rows = tile_count // TCOLS

    def assemble(values):
        shaped = values.reshape(slice_count, grid_rows, TCOLS, tile_size, tile_size)
        shaped = jnp.transpose(shaped, (0, 1, 3, 2, 4))
        return shaped.reshape(slice_count, grid_rows * tile_size, TCOLS * tile_size)

    def split_back(values):
        shaped = values.reshape(2, slice_count, grid_rows, tile_size, TCOLS, tile_size)
        shaped = jnp.transpose(shaped, (0, 1, 2, 4, 3, 5))
        return shaped.reshape(2, slice_count, tile_count, tile_size, tile_size)
    amplitude_full = assemble(amplitude)
    phase_full = assemble(phase_map)
    transmission = jnp.stack([amplitude_full * jnp.cos(phase_full), amplitude_full * jnp.sin(phase_full)])
    transmission = jnp.pad(transmission, ((0, 0), (0, 0), (RIM, RIM), (RIM, RIM)))
    tables = dft_tables(PROBE)
    operators = build_operators(propagator_phase, tables)
    starting = jnp.broadcast_to(probe_wave[:, None], (2, WAVES, PROBE, PROBE))

    def one_tile(buffer, inputs):
        tile_number, corners, observed = inputs
        corner = jnp.stack([tile_number // TCOLS * tile_size, tile_number % TCOLS * tile_size]).astype(jnp.int32)
        windows = (corners + corner[None, :] + RIM).astype(jnp.int32)
        patch_real, patch_imag = cut_patches(transmission, windows, PROBE)
        exit_wave, kept_real, kept_imag = forward_pass(starting, patch_real, patch_imag, operators, SLICE_DEV)
        backflow = farfield_residual(exit_wave, observed, tables)
        unused, grad_real, grad_imag = adjoint_pass(backflow, kept_real, kept_imag, patch_real, patch_imag, operators, SLICE_DEV)
        return (deposit(buffer, grad_real, grad_imag, windows), None)
    buffer = jnp.zeros(transmission.shape, jnp.float32)
    buffer, unused = lax.scan(one_tile, buffer, (jnp.arange(tile_count, dtype=jnp.int32), positions, measured))
    height = grid_rows * tile_size
    full_width = TCOLS * tile_size
    return split_back(buffer[:, :, RIM:RIM + height, RIM:RIM + full_width])
```

```python
import functools
import math

import jax
import jax.numpy as jnp
import numpy as np
from jax import lax
from jax.experimental import pallas as pl
from jax.experimental.pallas import tpu as pltpu
from jax.sharding import PartitionSpec as P

RIM = 64
LANES = 128
F32 = jnp.float32
BF16 = jnp.bfloat16
VMEM = pl.BlockSpec(memory_space=pltpu.VMEM)
SMEM = pl.BlockSpec(memory_space=pltpu.SMEM)


def call(body, out_shape, inputs, specs=None, scratch=(), flops=0, limit=24, name=None):
    out_specs = jax.tree.map(lambda _: VMEM, out_shape)
    moved = sum(x.size * x.dtype.itemsize for x in inputs)
    moved += sum(x.size * x.dtype.itemsize for x in jax.tree.leaves(out_shape))
    return pl.pallas_call(
        body,
        out_shape=out_shape,
        in_specs=specs or [VMEM] * len(inputs),
        out_specs=out_specs,
        scratch_shapes=list(scratch),
        compiler_params=pltpu.CompilerParams(vmem_limit_bytes=limit << 20),
        cost_estimate=pl.CostEstimate(flops=flops, bytes_accessed=moved, transcendentals=0),
        name=name,
    )(*inputs)


def sds(*shape, dtype=BF16):
    return jax.ShapeDtypeStruct(shape, dtype)


def sincos(x):
    y = x * 0.5
    q = y * y
    sine = 1.0
    for n in (11, 9, 7, 5, 3):
        sine = 1.0 - q * sine * (1.0 / (n * (n - 1)))
    sine = sine * y
    cosine = 1.0
    for n in (12, 10, 8, 6, 4, 2):
        cosine = 1.0 - q * cosine * (1.0 / (n * (n - 1)))
    return 2.0 * sine * cosine, 1.0 - 2.0 * sine * sine


def dft_tables(points):
    products = np.outer(np.arange(points), np.arange(points)) % points
    angles = products * (-2.0 * math.pi / points)
    scale = 1.0 / math.sqrt(points)
    return (np.cos(angles) * scale).astype(np.float32), (np.sin(angles) * scale).astype(np.float32)


def transmit_body(amp_ref, phase_ref, t_ref, up_ref, down_ref):
    size = amp_ref.shape[-1]
    for s in range(amp_ref.shape[0]):
        sine, cosine = sincos(phase_ref[s])
        amp = amp_ref[s]
        for part, value in enumerate((amp * cosine, amp * sine)):
            value = value.astype(BF16)
            t_ref[s, part] = value
            up_ref[s, part] = value[:RIM]
            down_ref[s, part] = value[size - RIM :]


def lane_halves(low, high):
    lane = lax.broadcasted_iota(jnp.int32, low.shape, 1)
    return jnp.where(lane < RIM, low, high)


def swap(x):
    return pltpu.roll(x, RIM, 1)


def column_body(t_ref, above_ref, below_ref, left_ref, right_ref):
    size = t_ref.shape[-1]
    for s in range(t_ref.shape[0]):
        for start, rows, ref in (
            (0, RIM, above_ref),
            (RIM, size, t_ref),
            (RIM + size, RIM, below_ref),
        ):
            dst = pl.ds(start, rows)
            real = ref[s, 0, :, :LANES].astype(F32)
            imag = ref[s, 1, :, :LANES].astype(F32)
            left_ref[s, dst, :] = lane_halves(real, swap(imag)).astype(BF16)
            real = ref[s, 0, :, size - LANES :].astype(F32)
            imag = ref[s, 1, :, size - LANES :].astype(F32)
            right_ref[s, dst, :] = lane_halves(swap(real), imag).astype(BF16)


def lane_place(column, size):
    tiles = (size + 2 * RIM) // LANES
    place = jnp.where(column < 0, column + size + 2 * RIM, column)
    first = place // LANES
    second = jnp.where(first == tiles - 1, 0, first + 1)
    return first, second, place % LANES


def cut_body(count, pos_ref, t_ref, above_ref, below_ref, lrim_ref, rrim_ref, *rest):
    outs, ext = rest[:count], rest[count]
    size = t_ref.shape[-1]
    slices = t_ref.shape[0]
    for s in range(slices):
        for part in range(2):
            for start, rows, ref in (
                (0, RIM, above_ref),
                (RIM, size, t_ref),
                (RIM + size, RIM, below_ref),
            ):
                for tile in range(size // LANES):
                    ext[tile, s, part, pl.ds(start, rows), :] = ref[
                        s, part, :, tile * LANES : (tile + 1) * LANES
                    ].astype(F32)
        left = lrim_ref[s].astype(F32)
        right = rrim_ref[s].astype(F32)
        ext[size // LANES, s, 0] = lane_halves(right, swap(left))
        ext[size // LANES, s, 1] = lane_halves(swap(right), left)
    depth = lax.axis_index("depth")
    for k in range(count):
        wave = lax.rem(depth + k, count)
        row = pos_ref[wave, 0] + RIM
        first, second, shift = lane_place(pos_ref[wave, 1], size)
        turn = lax.rem(LANES - shift, LANES)
        lane = lax.broadcasted_iota(jnp.int32, (LANES, LANES), 1)
        for s in range(slices):
            for part in range(2):
                low = pltpu.roll(ext[first, s, part, pl.ds(row, LANES), :], turn, 1)
                high = pltpu.roll(ext[second, s, part, pl.ds(row, LANES), :], turn, 1)
                outs[k][s, part] = jnp.where(lane < LANES - shift, low, high).astype(BF16)


def operator_body(phase_ref, dft_real_ref, dft_imag_ref, fwd_ref, bwd_ref):
    fr = dft_real_ref[...]
    fi = dft_imag_ref[...]
    n = fr.shape[0]

    def dot(a, b):
        return jnp.dot(a, b, precision=lax.Precision.HIGHEST, preferred_element_type=F32)

    def put(index, real, imag, flip):
        rt, it = real.T, imag.T
        plain = ((real, imag), (-imag, real))
        turned = ((rt, -it), (it, rt))
        for i in range(2):
            for j in range(2):
                rows, cols = pl.ds(i * n, n), pl.ds(j * n, n)
                value = (turned if flip else plain)[i][j]
                high = value.astype(BF16)
                fwd_ref[index, 0, rows, cols] = high
                fwd_ref[index, 1, rows, cols] = (value - high.astype(F32)).astype(BF16)
                bwd_ref[index, rows, cols] = (plain if flip else turned)[i][j].astype(BF16)

    for axis in range(2):
        sine, cosine = sincos(phase_ref[axis : axis + 1, :])
        er = fr * cosine - fi * sine
        ei = fr * sine + fi * cosine
        real = dot(er, fr) + dot(ei, fi)
        imag = dot(ei, fr) - dot(er, fi)
        put(axis, real, imag, axis == 0)
        put(2 + axis, er, ei, axis == 0)


def split(x):
    high = x.astype(BF16)
    return high, (x - high.astype(F32)).astype(BF16)


def mm(a, b):
    return jnp.dot(a, b, preferred_element_type=F32)


def left_fine(fwd_ref, index, real, imag):
    n = real.shape[0]
    high, low = split(jnp.concatenate([real, imag], axis=0))
    both = mm(fwd_ref[index, 0], jnp.concatenate([high, low], axis=1))
    out = both[:, :n] + both[:, n:] + mm(fwd_ref[index, 1], high)
    return out[:n], out[n:]


def right_fine(fwd_ref, index, real, imag):
    n = real.shape[0]
    high, low = split(jnp.concatenate([real, imag], axis=1))
    both = mm(jnp.concatenate([high, low], axis=0), fwd_ref[index, 0])
    out = both[:n] + both[n:] + mm(high, fwd_ref[index, 1])
    return out[:, :n], out[:, n:]


def left_plain(bwd_ref, index, real, imag):
    n = real.shape[0]
    out = mm(bwd_ref[index], jnp.concatenate([real, imag], axis=0).astype(BF16))
    return out[:n], out[n:]


def right_plain(bwd_ref, index, real, imag):
    n = real.shape[0]
    out = mm(jnp.concatenate([real, imag], axis=1).astype(BF16), bwd_ref[index])
    return out[:, :n], out[:, n:]


def wave_body(count, fwd_ref, bwd_ref, probe_ref, measured_ref, *rest):
    windows, outs = rest[:count], rest[count : 2 * count]
    patch, waves, grads = rest[2 * count :]
    depth = lax.axis_index("depth")
    slices = windows[0].shape[0]
    total = slices * count
    for k in range(count):
        group = lax.rem(depth + count - k, count)
        patch[group] = windows[k][...]

    def patch_of(s):
        group, local = s // slices, s % slices
        return patch[group, local, 0].astype(F32), patch[group, local, 1].astype(F32)

    def mix(s, wr, wi):
        pr, pi = patch_of(s)
        waves[s, 0] = wr
        waves[s, 1] = wi
        return pr * wr - pi * wi, pr * wi + pi * wr

    def forward(s, wave):
        half = left_fine(fwd_ref, 0, *mix(s, *wave))
        return right_fine(fwd_ref, 1, *half)

    wave = lax.fori_loop(0, total - 1, forward, (probe_ref[0], probe_ref[1]))
    half = left_fine(fwd_ref, 2, *mix(total - 1, *wave))
    far_real, far_imag = right_fine(fwd_ref, 3, *half)
    misfit = far_real * far_real + far_imag * far_imag - measured_ref[depth]
    half = left_plain(bwd_ref, 2, misfit * far_real, misfit * far_imag)
    spread = right_plain(bwd_ref, 3, *half)

    def contribute(s, sr, si):
        wr, wi = waves[s, 0], waves[s, 1]
        group, local = s // slices, s % slices
        grads[group, local, 0] = (wr * sr + wi * si).astype(BF16)
        grads[group, local, 1] = (wr * si - wi * sr).astype(BF16)

    def backward(step, spread):
        s = total - 1 - step
        sr, si = spread
        contribute(s, sr, si)
        pr, pi = patch_of(s)
        half = left_plain(bwd_ref, 0, pr * sr + pi * si, pr * si - pi * sr)
        return right_plain(bwd_ref, 1, *half)

    spread = lax.fori_loop(0, total - 1, backward, spread)
    contribute(0, *spread)
    for k in range(count):
        outs[k][...] = grads[lax.rem(depth + k, count)]


def deposit_body(count, pos_ref, *rest):
    grads = rest[:count]
    inner_ref, left_ref, right_ref, ext = rest[count:]
    size = inner_ref.shape[-1]
    tiles = ext.shape[0]
    slices = grads[0].shape[0]
    ext[...] = jnp.zeros_like(ext)
    depth = lax.axis_index("depth")
    for k in range(count):
        wave = lax.rem(depth + count - k, count)
        row = pos_ref[wave, 0] + RIM
        first, second, shift = lane_place(pos_ref[wave, 1], size)
        lane = lax.broadcasted_iota(jnp.int32, (LANES, LANES), 1)
        rows = pl.ds(row, LANES)
        for s in range(slices):
            for part in range(2):
                moved = pltpu.roll(grads[k][s, part].astype(F32), shift, 1)
                low = jnp.where(lane >= shift, moved, 0.0)
                ext[first, s, part, rows, :] += low
                ext[second, s, part, rows, :] += moved - low
    for s in range(slices):
        real, imag = ext[tiles - 1, s, 0], ext[tiles - 1, s, 1]
        right_ref[s] = lane_halves(real, swap(imag)).astype(BF16)
        left_ref[s] = lane_halves(swap(real), imag).astype(BF16)
        for part in range(2):
            for tile in range(tiles - 1):
                inner_ref[s, part, :, tile * LANES : (tile + 1) * LANES] = ext[tile, s, part]


def halves_added(inner_ref, left_ref, right_ref, s, part, rows):
    size = inner_ref.shape[-1]
    left = left_ref[s, rows, :].astype(F32)
    right = right_ref[s, rows, :].astype(F32)
    if part == 0:
        right = swap(right)
    else:
        left = swap(left)
    zero = jnp.zeros_like(left)
    first = inner_ref[s, part, rows, :LANES] + lane_halves(left, zero)
    last = inner_ref[s, part, rows, size - LANES :] + lane_halves(zero, right)
    return first, last


def row_body(inner_ref, left_ref, right_ref, up_ref, down_ref):
    size = inner_ref.shape[-1]
    height = inner_ref.shape[-2]
    for s in range(inner_ref.shape[0]):
        for part in range(2):
            for start, out in ((0, up_ref), (height - RIM, down_ref)):
                rows = pl.ds(start, RIM)
                first, last = halves_added(inner_ref, left_ref, right_ref, s, part, rows)
                out[s, part, :, :LANES] = first.astype(BF16)
                out[s, part, :, size - LANES :] = last.astype(BF16)


def finish_body(inner_ref, left_ref, right_ref, above_ref, below_ref, out_ref):
    size = inner_ref.shape[-1]
    for s in range(inner_ref.shape[0]):
        for part in range(2):
            for start in range(0, size, RIM):
                rows = pl.ds(RIM + start, RIM)
                pieces = halves_added(inner_ref, left_ref, right_ref, s, part, rows)
                for tile, piece in enumerate(pieces):
                    lanes = slice(tile * LANES, (tile + 1) * LANES)
                    if start == 0:
                        piece = piece + above_ref[s, part, :, lanes].astype(F32)
                    if start == size - RIM:
                        piece = piece + below_ref[s, part, :, lanes].astype(F32)
                    out_ref[part, s, start : start + RIM, lanes] = piece


def shards(amplitude, phase_map, probe_wave, propagator_phase, positions, measured):
    slices, size = amplitude.shape[0], amplitude.shape[-1]
    points = probe_wave.shape[-1]
    count = lax.axis_size("depth")
    tiles = lax.axis_size("tile")
    columns = max(2, tiles // 8)
    pos = positions[0]

    def row_shift(x, by):
        pairs = [(i, i + by * columns) for i in range(tiles) if 0 <= i + by * columns < tiles]
        return lax.ppermute(x, "tile", pairs)

    def column_shift(x, by):
        pairs = [(i, i + by) for i in range(tiles) if 0 <= i % columns + by < columns]
        return lax.ppermute(x, "tile", pairs)

    def depth_shift(x, by):
        return lax.ppermute(x, "depth", [(i, (i + by) % count) for i in range(count)])

    rim_rows = sds(slices, 2, RIM, size)
    rim_cols = sds(slices, size + 2 * RIM, LANES)
    window = sds(slices, 2, points, points)
    trans, up, down = call(
        transmit_body,
        (sds(slices, 2, size, size), rim_rows, rim_rows),
        (amplitude[:, 0], phase_map[:, 0]),
        flops=40 * 2 * size * size,
        name="transmit",
    )
    below = row_shift(up, -1)
    above = row_shift(down, 1)
    dft_real, dft_imag = dft_tables(points)
    fwd, bwd = call(
        operator_body,
        (sds(4, 2, 2 * points, 2 * points), sds(4, 2 * points, 2 * points)),
        (propagator_phase, jnp.asarray(dft_real), jnp.asarray(dft_imag)),
        flops=8 * 6 * 2 * points**3,
        name="operators",
    )
    left, right = call(
        column_body, (rim_cols, rim_cols), (trans, above, below), name="column_rims"
    )
    right_rim = column_shift(left, -1)
    left_rim = column_shift(right, 1)
    ext_tiles = (size + 2 * RIM) // LANES
    ext = pltpu.VMEM((ext_tiles, slices, 2, size + 2 * RIM, LANES), F32)
    windows = call(
        functools.partial(cut_body, count),
        (window,) * count,
        (pos, trans, above, below, left_rim, right_rim),
        specs=[SMEM] + [VMEM] * 5,
        scratch=(ext,),
        name="cut",
    )
    arrived = [windows[0]] + [depth_shift(windows[k], k) for k in range(1, count)]
    total = slices * count
    grads = call(
        functools.partial(wave_body, count),
        (window,) * count,
        (fwd, bwd, probe_wave, measured[0], *arrived),
        scratch=(
            pltpu.VMEM((count, slices, 2, points, points), BF16),
            pltpu.VMEM((total, 2, points, points), F32),
            pltpu.VMEM((count, slices, 2, points, points), BF16),
        ),
        flops=36 * 8 * 2 * points**3,
        name="waves",
    )
    returned = [grads[0]] + [depth_shift(grads[k], k) for k in range(1, count)]
    inner, left, right = call(
        functools.partial(deposit_body, count),
        (sds(slices, 2, size + 2 * RIM, size, dtype=F32), rim_cols, rim_cols),
        (pos, *returned),
        specs=[SMEM] + [VMEM] * count,
        scratch=(ext,),
        name="deposit",
    )
    from_right = column_shift(left, -1)
    from_left = column_shift(right, 1)
    up, down = call(
        row_body, (rim_rows, rim_rows), (inner, from_left, from_right), name="row_rims"
    )
    from_below = row_shift(up, -1)
    from_above = row_shift(down, 1)
    gradient = call(
        finish_body,
        sds(2, slices, size, size, dtype=F32),
        (inner, from_left, from_right, from_above, from_below),
        name="finish",
    )
    return gradient[:, :, None]


def solution(mesh):
    in_specs = (
        P("depth", "tile", None, None),
        P("depth", "tile", None, None),
        P(),
        P(),
        P("tile", None, None),
        P("tile", None, None, None),
    )
    out_specs = P(None, "depth", "tile", None, None)
    return jax.shard_map(shards, mesh=mesh, in_specs=in_specs, out_specs=out_specs, check_vma=False)
```

```python
import functools
import math

import jax
import jax.numpy as jnp
import numpy as np
from jax import lax
from jax.experimental import pallas as pl
from jax.experimental.pallas import tpu as pltpu
from jax.sharding import PartitionSpec as P

RIM = 64
LANES = 128
F32 = jnp.float32
BF16 = jnp.bfloat16
VMEM = pl.BlockSpec(memory_space=pltpu.VMEM)
SMEM = pl.BlockSpec(memory_space=pltpu.SMEM)
HBM = pl.BlockSpec(memory_space=pltpu.MemorySpace.HBM)


def call(body, out_shape, inputs, specs=None, outs=VMEM, scratch=(), flops=0, aliases=None, name=None):
    out_specs = jax.tree.map(lambda _: outs, out_shape)
    moved = sum(x.size * x.dtype.itemsize for x in inputs)
    moved += sum(x.size * x.dtype.itemsize for x in jax.tree.leaves(out_shape))
    return pl.pallas_call(
        body,
        out_shape=out_shape,
        in_specs=specs or [VMEM] * len(inputs),
        out_specs=out_specs,
        scratch_shapes=list(scratch),
        compiler_params=pltpu.CompilerParams(vmem_limit_bytes=24 << 20),
        input_output_aliases=aliases or {},
        cost_estimate=pl.CostEstimate(flops=flops, bytes_accessed=moved, transcendentals=0),
        name=name,
    )(*inputs)


def sds(*shape, dtype=BF16):
    return jax.ShapeDtypeStruct(shape, dtype)


def sincos(x):
    y = x * 0.5
    q = y * y
    sine = 1.0
    for n in (11, 9, 7, 5, 3):
        sine = 1.0 - q * sine * (1.0 / (n * (n - 1)))
    sine = sine * y
    cosine = 1.0
    for n in (12, 10, 8, 6, 4, 2):
        cosine = 1.0 - q * cosine * (1.0 / (n * (n - 1)))
    return 2.0 * sine * cosine, 1.0 - 2.0 * sine * sine


def dft_tables(points):
    products = np.outer(np.arange(points), np.arange(points)) % points
    angles = products * (-2.0 * math.pi / points)
    scale = 1.0 / math.sqrt(points)
    return (np.cos(angles) * scale).astype(np.float32), (np.sin(angles) * scale).astype(np.float32)


def odd_row(columns):
    return lax.rem(lax.axis_index("tile") // columns, 2) == 1


def odd_column():
    return lax.rem(lax.axis_index("tile"), 2) == 1


def rim_body(columns, amp_ref, phase_ref, first_ref, second_ref, held, sem):
    slices, size = amp_ref.shape[0], amp_ref.shape[-1]
    odd = odd_row(columns)
    copies = {}
    for block in range(2):
        top = odd if block == 0 else jnp.logical_not(odd)
        start = pl.multiple_of(jnp.where(top, 0, size - RIM), RIM)
        for s in range(slices):
            for i, ref in enumerate((phase_ref, amp_ref)):
                copy = pltpu.make_async_copy(
                    ref.at[s, pl.ds(start, RIM), :], held.at[block, s, i], sem.at[block, s, i]
                )
                copy.start()
                copies[block, s, i] = copy
    for block, out in enumerate((first_ref, second_ref)):
        for s in range(slices):
            copies[block, s, 0].wait()
            sine, cosine = sincos(held[block, s, 0])
            copies[block, s, 1].wait()
            amp = held[block, s, 1]
            out[s, 0] = (amp * cosine).astype(BF16)
            out[s, 1] = (amp * sine).astype(BF16)


def transmit_body(amp_ref, phase_ref, t_ref, held, sem):
    slices = amp_ref.shape[0]
    copies = []
    for s in range(slices):
        for i, ref in enumerate((phase_ref, amp_ref)):
            copies.append(pltpu.make_async_copy(ref.at[s], held.at[s, i], sem.at[s, i]))
            copies[-1].start()
    for s in range(slices):
        copies[2 * s].wait()
        copies[2 * s + 1].wait()
        sine, cosine = sincos(held[s, 0])
        amp = held[s, 1]
        t_ref[s, 0] = (amp * cosine).astype(BF16)
        t_ref[s, 1] = (amp * sine).astype(BF16)


def lane_halves(low, high):
    lane = lax.broadcasted_iota(jnp.int32, low.shape, 1)
    return jnp.where(lane < RIM, low, high)


def swap(x):
    return pltpu.roll(x, RIM, 1)


def column_body(columns, t_ref, row_first_ref, row_second_ref, first_ref, second_ref):
    size = t_ref.shape[-1]
    flip = odd_row(columns)
    odd = odd_column()
    for s in range(t_ref.shape[0]):
        for start, rows in ((0, RIM), (RIM, size), (RIM + size, RIM)):
            dst = pl.ds(start, rows)

            def load(part, lanes):
                if start == RIM:
                    return t_ref[s, part, :, lanes].astype(F32)
                first = row_first_ref[s, part, :, lanes].astype(F32)
                second = row_second_ref[s, part, :, lanes].astype(F32)
                return jnp.where(flip == (start == 0), first, second)

            low, high = slice(0, LANES), slice(size - LANES, size)
            left = lane_halves(load(0, low), swap(load(1, low)))
            right = lane_halves(swap(load(0, high)), load(1, high))
            first_ref[s, dst, :] = jnp.where(odd, right, left).astype(BF16)
            second_ref[s, dst, :] = jnp.where(odd, left, right).astype(BF16)


def extend_body(columns, t_ref, row_first_ref, row_second_ref, ext_ref):
    slices, size = t_ref.shape[0], t_ref.shape[-1]
    flip = odd_row(columns)
    for s in range(slices):
        for part in range(2):
            for tile in range(size // LANES):
                lanes = slice(tile * LANES, (tile + 1) * LANES)
                first = row_first_ref[s, part, :, lanes].astype(F32)
                second = row_second_ref[s, part, :, lanes].astype(F32)
                ext_ref[tile, s, part, :RIM] = jnp.where(flip, first, second)
                ext_ref[tile, s, part, RIM : RIM + size] = t_ref[s, part, :, lanes].astype(F32)
                ext_ref[tile, s, part, RIM + size :] = jnp.where(flip, second, first)


def lane_place(column, size):
    tiles = (size + 2 * RIM) // LANES
    place = jnp.where(column < 0, column + size + 2 * RIM, column)
    first = place // LANES
    second = jnp.where(first == tiles - 1, 0, first + 1)
    return first, second, place % LANES


def cut_body(count, size, pos_ref, rim_first_ref, rim_second_ref, ext_in, ext, *outs):
    del ext_in
    slices = ext.shape[1]
    odd = odd_column()
    for s in range(slices):
        first = rim_first_ref[s].astype(F32)
        second = rim_second_ref[s].astype(F32)
        left = jnp.where(odd, second, first)
        right = jnp.where(odd, first, second)
        ext[size // LANES, s, 0] = lane_halves(right, swap(left))
        ext[size // LANES, s, 1] = lane_halves(swap(right), left)
    depth = lax.axis_index("depth")
    for k in range(count):
        wave = depth ^ k
        row = pos_ref[wave, 0] + RIM
        first, second, shift = lane_place(pos_ref[wave, 1], size)
        turn = lax.rem(LANES - shift, LANES)
        lane = lax.broadcasted_iota(jnp.int32, (LANES, LANES), 1)
        for s in range(slices):
            for part in range(2):
                low = pltpu.roll(ext[first, s, part, pl.ds(row, LANES), :], turn, 1)
                high = pltpu.roll(ext[second, s, part, pl.ds(row, LANES), :], turn, 1)
                outs[k][s, part] = jnp.where(lane < LANES - shift, low, high).astype(BF16)


def operator_body(phase_ref, dft_real_ref, dft_imag_ref, fwd_ref, bwd_ref):
    fr = dft_real_ref[...]
    fi = dft_imag_ref[...]
    n = fr.shape[0]

    def dot(a, b):
        return jnp.dot(a, b, precision=lax.Precision.HIGHEST, preferred_element_type=F32)

    def put(index, real, imag, flip):
        rt, it = real.T, imag.T
        plain = ((real, imag), (-imag, real))
        turned = ((rt, -it), (it, rt))
        for i in range(2):
            for j in range(2):
                rows, cols = pl.ds(i * n, n), pl.ds(j * n, n)
                value = (turned if flip else plain)[i][j]
                high = value.astype(BF16)
                fwd_ref[index, 0, rows, cols] = high
                fwd_ref[index, 1, rows, cols] = (value - high.astype(F32)).astype(BF16)
                bwd_ref[index, rows, cols] = (plain if flip else turned)[i][j].astype(BF16)

    for axis in range(2):
        sine, cosine = sincos(phase_ref[axis : axis + 1, :])
        er = fr * cosine - fi * sine
        ei = fr * sine + fi * cosine
        real = dot(er, fr) + dot(ei, fi)
        imag = dot(ei, fr) - dot(er, fi)
        put(axis, real, imag, axis == 0)
        put(2 + axis, er, ei, axis == 0)


def split(x):
    high = x.astype(BF16)
    return high, (x - high.astype(F32)).astype(BF16)


def mm(a, b):
    return jnp.dot(a, b, preferred_element_type=F32)


def left_fine(fwd_ref, index, real, imag):
    n = real.shape[0]
    high, low = split(jnp.concatenate([real, imag], axis=0))
    both = mm(fwd_ref[index, 0], jnp.concatenate([high, low], axis=1))
    out = both[:, :n] + both[:, n:] + mm(fwd_ref[index, 1], high)
    return out[:n], out[n:]


def right_fine(fwd_ref, index, real, imag):
    n = real.shape[0]
    high, low = split(jnp.concatenate([real, imag], axis=1))
    both = mm(jnp.concatenate([high, low], axis=0), fwd_ref[index, 0])
    out = both[:n] + both[n:] + mm(high, fwd_ref[index, 1])
    return out[:, :n], out[:, n:]


def left_plain(bwd_ref, index, real, imag):
    n = real.shape[0]
    out = mm(bwd_ref[index], jnp.concatenate([real, imag], axis=0).astype(BF16))
    return out[:n], out[n:]


def right_plain(bwd_ref, index, real, imag):
    n = real.shape[0]
    out = mm(jnp.concatenate([real, imag], axis=1).astype(BF16), bwd_ref[index])
    return out[:, :n], out[:, n:]


def wave_body(count, fwd_ref, bwd_ref, probe_ref, measured_ref, *rest):
    windows, outs = rest[:count], rest[count : 2 * count]
    patch, waves, grads = rest[2 * count :]
    depth = lax.axis_index("depth")
    slices = windows[0].shape[0]
    total = slices * count
    for k in range(count):
        patch[depth ^ k] = windows[k][...]

    def patch_of(s):
        group, local = s // slices, s % slices
        return patch[group, local, 0].astype(F32), patch[group, local, 1].astype(F32)

    def mix(s, wr, wi):
        pr, pi = patch_of(s)
        waves[s, 0] = wr
        waves[s, 1] = wi
        return pr * wr - pi * wi, pr * wi + pi * wr

    def forward(s, wave):
        half = left_fine(fwd_ref, 0, *mix(s, *wave))
        return right_fine(fwd_ref, 1, *half)

    wave = lax.fori_loop(0, total - 1, forward, (probe_ref[0], probe_ref[1]))
    half = left_fine(fwd_ref, 2, *mix(total - 1, *wave))
    far_real, far_imag = right_fine(fwd_ref, 3, *half)
    misfit = far_real * far_real + far_imag * far_imag - measured_ref[depth]
    half = left_plain(bwd_ref, 2, misfit * far_real, misfit * far_imag)
    spread = right_plain(bwd_ref, 3, *half)

    def contribute(s, sr, si):
        wr, wi = waves[s, 0], waves[s, 1]
        group, local = s // slices, s % slices
        grads[group, local, 0] = (wr * sr + wi * si).astype(BF16)
        grads[group, local, 1] = (wr * si - wi * sr).astype(BF16)

    def backward(step, spread):
        s = total - 1 - step
        sr, si = spread
        contribute(s, sr, si)
        pr, pi = patch_of(s)
        half = left_plain(bwd_ref, 0, pr * sr + pi * si, pr * si - pi * sr)
        return right_plain(bwd_ref, 1, *half)

    spread = lax.fori_loop(0, total - 1, backward, spread)
    contribute(0, *spread)
    for k in range(count):
        outs[k][...] = grads[depth ^ k]


def deposit_body(count, size, pos_ref, *rest):
    grads = rest[:count]
    ext, first_ref, second_ref = rest[count:]
    tiles = ext.shape[0]
    slices = grads[0].shape[0]
    ext[...] = jnp.zeros_like(ext)
    depth = lax.axis_index("depth")
    odd = odd_column()
    for k in range(count):
        wave = depth ^ k
        row = pos_ref[wave, 0] + RIM
        first, second, shift = lane_place(pos_ref[wave, 1], size)
        lane = lax.broadcasted_iota(jnp.int32, (LANES, LANES), 1)
        rows = pl.ds(row, LANES)
        for s in range(slices):
            for part in range(2):
                moved = pltpu.roll(grads[k][s, part].astype(F32), shift, 1)
                low = jnp.where(lane >= shift, moved, 0.0)
                ext[first, s, part, rows, :] += low
                ext[second, s, part, rows, :] += moved - low
    for s in range(slices):
        real, imag = ext[tiles - 1, s, 0], ext[tiles - 1, s, 1]
        right = lane_halves(real, swap(imag))
        left = lane_halves(swap(real), imag)
        first_ref[s] = jnp.where(odd, right, left).astype(BF16)
        second_ref[s] = jnp.where(odd, left, right).astype(BF16)


def halves_added(odd, ext_ref, rim_first_ref, rim_second_ref, s, part, rows):
    first = rim_first_ref[s, rows, :].astype(F32)
    second = rim_second_ref[s, rows, :].astype(F32)
    left = jnp.where(odd, second, first)
    right = jnp.where(odd, first, second)
    if part == 0:
        right = swap(right)
    else:
        left = swap(left)
    last = ext_ref.shape[0] - 2
    zero = jnp.zeros_like(left)
    return (
        ext_ref[0, s, part, rows, :] + lane_halves(left, zero),
        ext_ref[last, s, part, rows, :] + lane_halves(zero, right),
    )


def row_body(columns, ext_ref, rim_first_ref, rim_second_ref, first_ref, second_ref):
    height = ext_ref.shape[-2]
    odd = odd_column()
    flip = odd_row(columns)
    for s in range(ext_ref.shape[1]):
        for part in range(2):
            refs = (odd, ext_ref, rim_first_ref, rim_second_ref, s, part)
            above = halves_added(*refs, pl.ds(0, RIM))
            below = halves_added(*refs, pl.ds(height - RIM, RIM))
            for tile in range(2):
                lanes = slice(tile * LANES, (tile + 1) * LANES)
                up, down = above[tile], below[tile]
                first_ref[s, part, :, lanes] = jnp.where(flip, up, down).astype(BF16)
                second_ref[s, part, :, lanes] = jnp.where(flip, down, up).astype(BF16)


def put_rows(out_ref, held, sem, blocks):
    copies = []
    for part in range(out_ref.shape[0]):
        for s in range(out_ref.shape[1]):
            at = 0
            for i, (start, rows) in enumerate(blocks):
                copy = pltpu.make_async_copy(
                    held.at[part, s, pl.ds(at, rows), :],
                    out_ref.at[part, s, pl.ds(start, rows), :],
                    sem.at[part, s, i],
                )
                copies.append(copy)
                at += rows
    return copies


def middle_body(ext_ref, rim_first_ref, rim_second_ref, out_ref, held, sem):
    size = out_ref.shape[-1]
    odd = odd_column()
    copies = put_rows(out_ref, held, sem, ((RIM, size - 2 * RIM),))
    for part in range(2):
        for s in range(ext_ref.shape[1]):
            rows = pl.ds(2 * RIM, size - 2 * RIM)
            pieces = halves_added(odd, ext_ref, rim_first_ref, rim_second_ref, s, part, rows)
            for tile, piece in enumerate(pieces):
                held[part, s, :, tile * LANES : (tile + 1) * LANES] = piece
    for copy in copies:
        copy.start()
    for copy in copies:
        copy.wait()


def edge_body(columns, ext_ref, rim_first_ref, rim_second_ref, *rest):
    row_first_ref, row_second_ref, out_in, out_ref, held, sem = rest
    del out_in
    size = out_ref.shape[-1]
    odd = odd_column()
    flip = odd_row(columns)
    blocks = ((0, RIM), (size - RIM, RIM))
    copies = put_rows(out_ref, held, sem, blocks)
    for part in range(2):
        for s in range(ext_ref.shape[1]):
            for i, (start, rows) in enumerate(blocks):
                refs = (odd, ext_ref, rim_first_ref, rim_second_ref, s, part)
                pieces = halves_added(*refs, pl.ds(RIM + start, rows))
                for tile, piece in enumerate(pieces):
                    lanes = slice(tile * LANES, (tile + 1) * LANES)
                    first = row_first_ref[s, part, :, lanes].astype(F32)
                    second = row_second_ref[s, part, :, lanes].astype(F32)
                    piece = piece + jnp.where(flip == (start == 0), first, second)
                    held[part, s, i * RIM : (i + 1) * RIM, lanes] = piece
                copies[(part * ext_ref.shape[1] + s) * 2 + i].start()
    for copy in copies:
        copy.wait()


def shards(amplitude, phase_map, probe_wave, propagator_phase, positions, measured):
    slices, size = amplitude.shape[0], amplitude.shape[-1]
    points = probe_wave.shape[-1]
    count = lax.axis_size("depth")
    tiles = lax.axis_size("tile")
    columns = max(2, tiles // 8)
    pos = positions[0]

    def row_swap(x, odd):
        low = [i for i in range(tiles - columns) if i // columns % 2 == odd]
        pairs = [(i, i + columns) for i in low] + [(i + columns, i) for i in low]
        return lax.ppermute(x, "tile", pairs)

    def column_swap(x, odd):
        low = [i for i in range(tiles) if i % 2 == odd and i % columns + 1 < columns]
        pairs = [(i, i + 1) for i in low] + [(i + 1, i) for i in low]
        return lax.ppermute(x, "tile", pairs)

    def depth_swap(x, by):
        return lax.ppermute(x, "depth", [(i, i ^ by) for i in range(count)])

    rim_rows = sds(slices, 2, RIM, size)
    rim_cols = sds(slices, size + 2 * RIM, LANES)
    window = sds(slices, 2, points, points)
    ext = sds((size + 2 * RIM) // LANES, slices, 2, size + 2 * RIM, LANES, dtype=F32)
    amplitude, phase_map = amplitude[:, 0], phase_map[:, 0]
    first, second = call(
        functools.partial(rim_body, columns),
        (rim_rows, rim_rows),
        (amplitude, phase_map),
        specs=[HBM, HBM],
        scratch=(
            pltpu.VMEM((2, slices, 2, RIM, size), F32),
            pltpu.SemaphoreType.DMA((2, slices, 2)),
        ),
        flops=40 * 4 * RIM * size,
        name="row_rims_out",
    )
    rows = row_swap(first, 0), row_swap(second, 1)
    trans = call(
        transmit_body,
        sds(slices, 2, size, size),
        (amplitude, phase_map),
        specs=[HBM, HBM],
        scratch=(pltpu.VMEM((slices, 2, size, size), F32), pltpu.SemaphoreType.DMA((slices, 2))),
        flops=40 * 2 * size * size,
        name="transmit",
    )
    dft_real, dft_imag = dft_tables(points)
    fwd, bwd = call(
        operator_body,
        (sds(4, 2, 2 * points, 2 * points), sds(4, 2 * points, 2 * points)),
        (propagator_phase, jnp.asarray(dft_real), jnp.asarray(dft_imag)),
        flops=8 * 6 * 2 * points**3,
        name="operators",
    )
    first, second = call(
        functools.partial(column_body, columns),
        (rim_cols, rim_cols),
        (trans, *rows),
        name="column_rims_out",
    )
    cols = column_swap(first, 1), column_swap(second, 0)
    extended = call(functools.partial(extend_body, columns), ext, (trans, *rows), name="extend")
    windows = call(
        functools.partial(cut_body, count, size),
        (ext,) + (window,) * count,
        (pos, *cols, extended),
        specs=[SMEM] + [VMEM] * 3,
        aliases={3: 0},
        name="cut",
    )[1:]
    arrived = [windows[0]] + [depth_swap(windows[k], k) for k in range(1, count)]
    total = slices * count
    grads = call(
        functools.partial(wave_body, count),
        (window,) * count,
        (fwd, bwd, probe_wave, measured[0], *arrived),
        scratch=(
            pltpu.VMEM((count, slices, 2, points, points), BF16),
            pltpu.VMEM((total, 2, points, points), F32),
            pltpu.VMEM((count, slices, 2, points, points), BF16),
        ),
        flops=36 * 8 * 2 * points**3,
        name="waves",
    )
    returned = [grads[0]] + [depth_swap(grads[k], k) for k in range(1, count)]
    summed, first, second = call(
        functools.partial(deposit_body, count, size),
        (ext, rim_cols, rim_cols),
        (pos, *returned),
        specs=[SMEM] + [VMEM] * count,
        name="deposit",
    )
    cols = column_swap(first, 1), column_swap(second, 0)
    first, second = call(
        functools.partial(row_body, columns),
        (rim_rows, rim_rows),
        (summed, *cols),
        name="row_rims_back",
    )
    rows = row_swap(first, 0), row_swap(second, 1)
    gradient = sds(2, slices, size, size, dtype=F32)
    middle = call(
        middle_body,
        gradient,
        (summed, *cols),
        outs=HBM,
        scratch=(
            pltpu.VMEM((2, slices, size - 2 * RIM, size), F32),
            pltpu.SemaphoreType.DMA((2, slices, 1)),
        ),
        name="middle_rows",
    )
    gradient = call(
        functools.partial(edge_body, columns),
        gradient,
        (summed, *cols, *rows, middle),
        specs=[VMEM] * 5 + [HBM],
        outs=HBM,
        scratch=(
            pltpu.VMEM((2, slices, 2 * RIM, size), F32),
            pltpu.SemaphoreType.DMA((2, slices, 2)),
        ),
        aliases={5: 0},
        name="edge_rows",
    )
    return gradient[:, :, None]


def solution(mesh):
    in_specs = (
        P("depth", "tile", None, None),
        P("depth", "tile", None, None),
        P(),
        P(),
        P("tile", None, None),
        P("tile", None, None, None),
    )
    out_specs = P(None, "depth", "tile", None, None)
    return jax.shard_map(shards, mesh=mesh, in_specs=in_specs, out_specs=out_specs, check_vma=False)
```

```python
import functools
import math

import jax
import jax.numpy as jnp
import numpy as np
from jax import lax
from jax.experimental import pallas as pl
from jax.experimental.pallas import tpu as pltpu
from jax.sharding import PartitionSpec as P

RIM = 64
LANES = 128
F32 = jnp.float32
BF16 = jnp.bfloat16
VMEM = pl.BlockSpec(memory_space=pltpu.VMEM)
SMEM = pl.BlockSpec(memory_space=pltpu.SMEM)
HBM = pl.BlockSpec(memory_space=pltpu.MemorySpace.HBM)


def call(body, out_shape, inputs, specs=None, outs=VMEM, scratch=(), flops=0, aliases=None, name=None):
    out_specs = jax.tree.map(lambda _: outs, out_shape)
    moved = sum(x.size * x.dtype.itemsize for x in inputs)
    moved += sum(x.size * x.dtype.itemsize for x in jax.tree.leaves(out_shape))
    return pl.pallas_call(
        body,
        out_shape=out_shape,
        in_specs=specs or [VMEM] * len(inputs),
        out_specs=out_specs,
        scratch_shapes=list(scratch),
        compiler_params=pltpu.CompilerParams(vmem_limit_bytes=24 << 20),
        input_output_aliases=aliases or {},
        cost_estimate=pl.CostEstimate(flops=flops, bytes_accessed=moved, transcendentals=0),
        name=name,
    )(*inputs)


def sds(*shape, dtype=BF16):
    return jax.ShapeDtypeStruct(shape, dtype)


def sincos(x):
    y = x * 0.5
    q = y * y
    sine = 1.0
    for n in (11, 9, 7, 5, 3):
        sine = 1.0 - q * sine * (1.0 / (n * (n - 1)))
    sine = sine * y
    cosine = 1.0
    for n in (12, 10, 8, 6, 4, 2):
        cosine = 1.0 - q * cosine * (1.0 / (n * (n - 1)))
    return 2.0 * sine * cosine, 1.0 - 2.0 * sine * sine


def dft_tables(points):
    products = np.outer(np.arange(points), np.arange(points)) % points
    angles = products * (-2.0 * math.pi / points)
    scale = 1.0 / math.sqrt(points)
    return (np.cos(angles) * scale).astype(np.float32), (np.sin(angles) * scale).astype(np.float32)


def odd_row(columns):
    return lax.rem(lax.axis_index("tile") // columns, 2) == 1


def odd_column():
    return lax.rem(lax.axis_index("tile"), 2) == 1


def rim_body(columns, amp_ref, phase_ref, first_ref, second_ref, held, sem):
    slices, size = amp_ref.shape[0], amp_ref.shape[-1]
    odd = odd_row(columns)
    copies = {}
    for block in range(2):
        top = odd if block == 0 else jnp.logical_not(odd)
        start = pl.multiple_of(jnp.where(top, 0, size - RIM), RIM)
        for s in range(slices):
            for i, ref in enumerate((phase_ref, amp_ref)):
                copy = pltpu.make_async_copy(
                    ref.at[s, pl.ds(start, RIM), :], held.at[block, s, i], sem.at[block, s, i]
                )
                copy.start()
                copies[block, s, i] = copy
    for block, out in enumerate((first_ref, second_ref)):
        for s in range(slices):
            copies[block, s, 0].wait()
            sine, cosine = sincos(held[block, s, 0])
            copies[block, s, 1].wait()
            amp = held[block, s, 1]
            out[s, 0] = (amp * cosine).astype(BF16)
            out[s, 1] = (amp * sine).astype(BF16)


def transmit_body(amp_ref, phase_ref, t_ref, held, sem):
    slices = amp_ref.shape[0]
    copies = []
    for s in range(slices):
        for i, ref in enumerate((phase_ref, amp_ref)):
            copies.append(pltpu.make_async_copy(ref.at[s], held.at[s, i], sem.at[s, i]))
            copies[-1].start()
    for s in range(slices):
        copies[2 * s].wait()
        copies[2 * s + 1].wait()
        sine, cosine = sincos(held[s, 0])
        amp = held[s, 1]
        t_ref[s, 0] = (amp * cosine).astype(BF16)
        t_ref[s, 1] = (amp * sine).astype(BF16)


def lane_halves(low, high):
    lane = lax.broadcasted_iota(jnp.int32, low.shape, 1)
    return jnp.where(lane < RIM, low, high)


def swap(x):
    return pltpu.roll(x, RIM, 1)


def column_body(columns, t_ref, row_first_ref, row_second_ref, first_ref, second_ref):
    size = t_ref.shape[-1]
    flip = odd_row(columns)
    odd = odd_column()
    for s in range(t_ref.shape[0]):
        for start, rows in ((0, RIM), (RIM, size), (RIM + size, RIM)):
            dst = pl.ds(start, rows)

            def load(part, lanes):
                if start == RIM:
                    return t_ref[s, part, :, lanes].astype(F32)
                first = row_first_ref[s, part, :, lanes].astype(F32)
                second = row_second_ref[s, part, :, lanes].astype(F32)
                return jnp.where(flip == (start == 0), first, second)

            low, high = slice(0, LANES), slice(size - LANES, size)
            left = lane_halves(load(0, low), swap(load(1, low)))
            right = lane_halves(swap(load(0, high)), load(1, high))
            first_ref[s, dst, :] = jnp.where(odd, right, left).astype(BF16)
            second_ref[s, dst, :] = jnp.where(odd, left, right).astype(BF16)


def extend_body(columns, t_ref, row_first_ref, row_second_ref, ext_ref):
    slices, size = t_ref.shape[0], t_ref.shape[-1]
    flip = odd_row(columns)
    for s in range(slices):
        for part in range(2):
            for tile in range(size // LANES):
                lanes = slice(tile * LANES, (tile + 1) * LANES)
                first = row_first_ref[s, part, :, lanes].astype(F32)
                second = row_second_ref[s, part, :, lanes].astype(F32)
                ext_ref[tile, s, part, :RIM] = jnp.where(flip, first, second)
                ext_ref[tile, s, part, RIM : RIM + size] = t_ref[s, part, :, lanes].astype(F32)
                ext_ref[tile, s, part, RIM + size :] = jnp.where(flip, second, first)


def lane_place(column, size):
    tiles = (size + 2 * RIM) // LANES
    place = jnp.where(column < 0, column + size + 2 * RIM, column)
    first = place // LANES
    second = jnp.where(first == tiles - 1, 0, first + 1)
    return first, second, place % LANES


def cut_body(count, size, pos_ref, rim_first_ref, rim_second_ref, ext_in, ext, *outs):
    del ext_in
    slices = ext.shape[1]
    odd = odd_column()
    for s in range(slices):
        first = rim_first_ref[s].astype(F32)
        second = rim_second_ref[s].astype(F32)
        left = jnp.where(odd, second, first)
        right = jnp.where(odd, first, second)
        ext[size // LANES, s, 0] = lane_halves(right, swap(left))
        ext[size // LANES, s, 1] = lane_halves(swap(right), left)
    depth = lax.axis_index("depth")
    for k in range(count):
        wave = depth ^ k
        row = pos_ref[wave, 0] + RIM
        first, second, shift = lane_place(pos_ref[wave, 1], size)
        turn = lax.rem(LANES - shift, LANES)
        lane = lax.broadcasted_iota(jnp.int32, (LANES, LANES), 1)
        for s in range(slices):
            for part in range(2):
                low = pltpu.roll(ext[first, s, part, pl.ds(row, LANES), :], turn, 1)
                high = pltpu.roll(ext[second, s, part, pl.ds(row, LANES), :], turn, 1)
                outs[k][s, part] = jnp.where(lane < LANES - shift, low, high).astype(BF16)


def operator_body(phase_ref, dft_real_ref, dft_imag_ref, fwd_ref, bwd_ref):
    fr = dft_real_ref[...]
    fi = dft_imag_ref[...]
    n = fr.shape[0]

    def dot(a, b):
        return jnp.dot(a, b, precision=lax.Precision.HIGHEST, preferred_element_type=F32)

    def put(index, real, imag, flip):
        rt, it = real.T, imag.T
        plain = ((real, imag), (-imag, real))
        turned = ((rt, -it), (it, rt))
        for i in range(2):
            for j in range(2):
                rows, cols = pl.ds(i * n, n), pl.ds(j * n, n)
                value = (turned if flip else plain)[i][j]
                high = value.astype(BF16)
                fwd_ref[index, 0, rows, cols] = high
                fwd_ref[index, 1, rows, cols] = (value - high.astype(F32)).astype(BF16)
                bwd_ref[index, rows, cols] = (plain if flip else turned)[i][j].astype(BF16)

    for axis in range(2):
        sine, cosine = sincos(phase_ref[axis : axis + 1, :])
        er = fr * cosine - fi * sine
        ei = fr * sine + fi * cosine
        real = dot(er, fr) + dot(ei, fi)
        imag = dot(ei, fr) - dot(er, fi)
        put(axis, real, imag, axis == 0)
        put(2 + axis, er, ei, axis == 0)


def split(x):
    high = x.astype(BF16)
    return high, (x - high.astype(F32)).astype(BF16)


def mm(a, b):
    return jnp.dot(a, b, preferred_element_type=F32)


def left_fine(fwd_ref, index, real, imag):
    n = real.shape[0]
    high, low = split(jnp.concatenate([real, imag], axis=0))
    both = mm(fwd_ref[index, 0], jnp.concatenate([high, low], axis=1))
    out = both[:, :n] + both[:, n:] + mm(fwd_ref[index, 1], high)
    return out[:n], out[n:]


def right_fine(fwd_ref, index, real, imag):
    n = real.shape[0]
    high, low = split(jnp.concatenate([real, imag], axis=1))
    both = mm(jnp.concatenate([high, low], axis=0), fwd_ref[index, 0])
    out = both[:n] + both[n:] + mm(high, fwd_ref[index, 1])
    return out[:, :n], out[:, n:]


def left_plain(bwd_ref, index, real, imag):
    n = real.shape[0]
    out = mm(bwd_ref[index], jnp.concatenate([real, imag], axis=0).astype(BF16))
    return out[:n], out[n:]


def right_plain(bwd_ref, index, real, imag):
    n = real.shape[0]
    out = mm(jnp.concatenate([real, imag], axis=1).astype(BF16), bwd_ref[index])
    return out[:, :n], out[:, n:]


def wave_body(count, fwd_ref, bwd_ref, probe_ref, measured_ref, *rest):
    windows, outs = rest[:count], rest[count : 2 * count]
    patch, waves, grads = rest[2 * count :]
    depth = lax.axis_index("depth")
    slices = windows[0].shape[0]
    total = slices * count
    for k in range(count):
        patch[depth ^ k] = windows[k][...]

    def patch_of(s):
        group, local = s // slices, s % slices
        return patch[group, local, 0].astype(F32), patch[group, local, 1].astype(F32)

    def mix(s, wr, wi):
        pr, pi = patch_of(s)
        waves[s, 0] = wr
        waves[s, 1] = wi
        return pr * wr - pi * wi, pr * wi + pi * wr

    def forward(s, wave):
        half = left_fine(fwd_ref, 0, *mix(s, *wave))
        return right_fine(fwd_ref, 1, *half)

    wave = lax.fori_loop(0, total - 1, forward, (probe_ref[0], probe_ref[1]))
    half = left_fine(fwd_ref, 2, *mix(total - 1, *wave))
    far_real, far_imag = right_fine(fwd_ref, 3, *half)
    misfit = far_real * far_real + far_imag * far_imag - measured_ref[depth]
    half = left_plain(bwd_ref, 2, misfit * far_real, misfit * far_imag)
    spread = right_plain(bwd_ref, 3, *half)

    def contribute(s, sr, si):
        wr, wi = waves[s, 0], waves[s, 1]
        group, local = s // slices, s % slices
        grads[group, local, 0] = (wr * sr + wi * si).astype(BF16)
        grads[group, local, 1] = (wr * si - wi * sr).astype(BF16)

    def backward(step, spread):
        s = total - 1 - step
        sr, si = spread
        contribute(s, sr, si)
        pr, pi = patch_of(s)
        half = left_plain(bwd_ref, 0, pr * sr + pi * si, pr * si - pi * sr)
        return right_plain(bwd_ref, 1, *half)

    spread = lax.fori_loop(0, total - 1, backward, spread)
    contribute(0, *spread)
    for k in range(count):
        outs[k][...] = grads[depth ^ k]


def deposit_body(count, size, pos_ref, *rest):
    grads = rest[:count]
    ext, first_ref, second_ref = rest[count:]
    tiles = ext.shape[0]
    slices = grads[0].shape[0]
    ext[...] = jnp.zeros_like(ext)
    depth = lax.axis_index("depth")
    odd = odd_column()
    for k in range(count):
        wave = depth ^ k
        row = pos_ref[wave, 0] + RIM
        first, second, shift = lane_place(pos_ref[wave, 1], size)
        lane = lax.broadcasted_iota(jnp.int32, (LANES, LANES), 1)
        rows = pl.ds(row, LANES)
        for s in range(slices):
            for part in range(2):
                moved = pltpu.roll(grads[k][s, part].astype(F32), shift, 1)
                low = jnp.where(lane >= shift, moved, 0.0)
                ext[first, s, part, rows, :] += low
                ext[second, s, part, rows, :] += moved - low
    for s in range(slices):
        real, imag = ext[tiles - 1, s, 0], ext[tiles - 1, s, 1]
        right = lane_halves(real, swap(imag))
        left = lane_halves(swap(real), imag)
        first_ref[s] = jnp.where(odd, right, left).astype(BF16)
        second_ref[s] = jnp.where(odd, left, right).astype(BF16)


def halves_added(odd, ext_ref, rim_first_ref, rim_second_ref, s, part, rows):
    first = rim_first_ref[s, rows, :].astype(F32)
    second = rim_second_ref[s, rows, :].astype(F32)
    left = jnp.where(odd, second, first)
    right = jnp.where(odd, first, second)
    if part == 0:
        right = swap(right)
    else:
        left = swap(left)
    last = ext_ref.shape[0] - 2
    zero = jnp.zeros_like(left)
    return (
        ext_ref[0, s, part, rows, :] + lane_halves(left, zero),
        ext_ref[last, s, part, rows, :] + lane_halves(zero, right),
    )


def row_body(columns, ext_ref, rim_first_ref, rim_second_ref, first_ref, second_ref):
    height = ext_ref.shape[-2]
    odd = odd_column()
    flip = odd_row(columns)
    for s in range(ext_ref.shape[1]):
        for part in range(2):
            refs = (odd, ext_ref, rim_first_ref, rim_second_ref, s, part)
            above = halves_added(*refs, pl.ds(0, RIM))
            below = halves_added(*refs, pl.ds(height - RIM, RIM))
            for tile in range(2):
                lanes = slice(tile * LANES, (tile + 1) * LANES)
                up, down = above[tile], below[tile]
                first_ref[s, part, :, lanes] = jnp.where(flip, up, down).astype(BF16)
                second_ref[s, part, :, lanes] = jnp.where(flip, down, up).astype(BF16)


def put_rows(out_ref, held, sem, blocks):
    copies = []
    for part in range(out_ref.shape[0]):
        for s in range(out_ref.shape[1]):
            at = 0
            for i, (start, rows) in enumerate(blocks):
                copy = pltpu.make_async_copy(
                    held.at[part, s, pl.ds(at, rows), :],
                    out_ref.at[part, s, pl.ds(start, rows), :],
                    sem.at[part, s, i],
                )
                copies.append(copy)
                at += rows
    return copies


def middle_body(ext_ref, rim_first_ref, rim_second_ref, out_ref, held, sem):
    size = out_ref.shape[-1]
    odd = odd_column()
    copies = put_rows(out_ref, held, sem, ((RIM, size - 2 * RIM),))
    for part in range(2):
        for s in range(ext_ref.shape[1]):
            rows = pl.ds(2 * RIM, size - 2 * RIM)
            pieces = halves_added(odd, ext_ref, rim_first_ref, rim_second_ref, s, part, rows)
            for tile, piece in enumerate(pieces):
                held[part, s, :, tile * LANES : (tile + 1) * LANES] = piece
    for copy in copies:
        copy.start()
    for copy in copies:
        copy.wait()


def edge_body(columns, ext_ref, rim_first_ref, rim_second_ref, *rest):
    row_first_ref, row_second_ref, out_in, out_ref, held, sem = rest
    del out_in
    size = out_ref.shape[-1]
    odd = odd_column()
    flip = odd_row(columns)
    blocks = ((0, RIM), (size - RIM, RIM))
    copies = put_rows(out_ref, held, sem, blocks)
    for part in range(2):
        for s in range(ext_ref.shape[1]):
            for i, (start, rows) in enumerate(blocks):
                refs = (odd, ext_ref, rim_first_ref, rim_second_ref, s, part)
                pieces = halves_added(*refs, pl.ds(RIM + start, rows))
                for tile, piece in enumerate(pieces):
                    lanes = slice(tile * LANES, (tile + 1) * LANES)
                    first = row_first_ref[s, part, :, lanes].astype(F32)
                    second = row_second_ref[s, part, :, lanes].astype(F32)
                    piece = piece + jnp.where(flip == (start == 0), first, second)
                    held[part, s, i * RIM : (i + 1) * RIM, lanes] = piece
                copies[(part * ext_ref.shape[1] + s) * 2 + i].start()
    for copy in copies:
        copy.wait()


def shards(amplitude, phase_map, probe_wave, propagator_phase, positions, measured):
    slices, size = amplitude.shape[0], amplitude.shape[-1]
    points = probe_wave.shape[-1]
    count = lax.axis_size("depth")
    tiles = lax.axis_size("tile")
    columns = max(2, tiles // 8)
    pos = positions[0]

    def row_swap(x, odd):
        low = [i for i in range(tiles - columns) if i // columns % 2 == odd]
        pairs = [(i, i + columns) for i in low] + [(i + columns, i) for i in low]
        return lax.ppermute(x, "tile", pairs)

    def column_swap(x, odd):
        low = [i for i in range(tiles) if i % 2 == odd and i % columns + 1 < columns]
        pairs = [(i, i + 1) for i in low] + [(i + 1, i) for i in low]
        return lax.ppermute(x, "tile", pairs)

    def depth_swap(x, by):
        return lax.ppermute(x, "depth", [(i, i ^ by) for i in range(count)])

    rim_rows = sds(slices, 2, RIM, size)
    rim_cols = sds(slices, size + 2 * RIM, LANES)
    window = sds(slices, 2, points, points)
    ext = sds((size + 2 * RIM) // LANES, slices, 2, size + 2 * RIM, LANES, dtype=F32)
    amplitude, phase_map = (
        pltpu.with_memory_space_constraint(x[:, 0], pltpu.MemorySpace.HBM)
        for x in (amplitude, phase_map)
    )
    first, second = call(
        functools.partial(rim_body, columns),
        (rim_rows, rim_rows),
        (amplitude, phase_map),
        specs=[HBM, HBM],
        scratch=(
            pltpu.VMEM((2, slices, 2, RIM, size), F32),
            pltpu.SemaphoreType.DMA((2, slices, 2)),
        ),
        flops=40 * 4 * RIM * size,
        name="row_rims_out",
    )
    rows = row_swap(first, 0), row_swap(second, 1)
    trans = call(
        transmit_body,
        sds(slices, 2, size, size),
        (amplitude, phase_map),
        specs=[HBM, HBM],
        scratch=(pltpu.VMEM((slices, 2, size, size), F32), pltpu.SemaphoreType.DMA((slices, 2))),
        flops=40 * 2 * size * size,
        name="transmit",
    )
    dft_real, dft_imag = dft_tables(points)
    fwd, bwd = call(
        operator_body,
        (sds(4, 2, 2 * points, 2 * points), sds(4, 2 * points, 2 * points)),
        (propagator_phase, jnp.asarray(dft_real), jnp.asarray(dft_imag)),
        flops=8 * 6 * 2 * points**3,
        name="operators",
    )
    first, second = call(
        functools.partial(column_body, columns),
        (rim_cols, rim_cols),
        (trans, *rows),
        name="column_rims_out",
    )
    cols = column_swap(first, 1), column_swap(second, 0)
    extended = call(functools.partial(extend_body, columns), ext, (trans, *rows), name="extend")
    windows = call(
        functools.partial(cut_body, count, size),
        (ext,) + (window,) * count,
        (pos, *cols, extended),
        specs=[SMEM] + [VMEM] * 3,
        aliases={3: 0},
        name="cut",
    )[1:]
    arrived = [windows[0]] + [depth_swap(windows[k], k) for k in range(1, count)]
    total = slices * count
    grads = call(
        functools.partial(wave_body, count),
        (window,) * count,
        (fwd, bwd, probe_wave, measured[0], *arrived),
        scratch=(
            pltpu.VMEM((count, slices, 2, points, points), BF16),
            pltpu.VMEM((total, 2, points, points), F32),
            pltpu.VMEM((count, slices, 2, points, points), BF16),
        ),
        flops=36 * 8 * 2 * points**3,
        name="waves",
    )
    returned = [grads[0]] + [depth_swap(grads[k], k) for k in range(1, count)]
    summed, first, second = call(
        functools.partial(deposit_body, count, size),
        (ext, rim_cols, rim_cols),
        (pos, *returned),
        specs=[SMEM] + [VMEM] * count,
        name="deposit",
    )
    cols = column_swap(first, 1), column_swap(second, 0)
    first, second = call(
        functools.partial(row_body, columns),
        (rim_rows, rim_rows),
        (summed, *cols),
        name="row_rims_back",
    )
    rows = row_swap(first, 0), row_swap(second, 1)
    gradient = sds(2, slices, size, size, dtype=F32)
    middle = call(
        middle_body,
        gradient,
        (summed, *cols),
        outs=HBM,
        scratch=(
            pltpu.VMEM((2, slices, size - 2 * RIM, size), F32),
            pltpu.SemaphoreType.DMA((2, slices, 1)),
        ),
        name="middle_rows",
    )
    gradient = call(
        functools.partial(edge_body, columns),
        gradient,
        (summed, *cols, *rows, middle),
        specs=[VMEM] * 5 + [HBM],
        outs=HBM,
        scratch=(
            pltpu.VMEM((2, slices, 2 * RIM, size), F32),
            pltpu.SemaphoreType.DMA((2, slices, 2)),
        ),
        aliases={5: 0},
        name="edge_rows",
    )
    return gradient[:, :, None]


def solution(mesh):
    in_specs = (
        P("depth", "tile", None, None),
        P("depth", "tile", None, None),
        P(),
        P(),
        P("tile", None, None),
        P("tile", None, None, None),
    )
    out_specs = P(None, "depth", "tile", None, None)
    return jax.shard_map(shards, mesh=mesh, in_specs=in_specs, out_specs=out_specs, check_vma=False)
```

```python
import functools
import math

import jax
import jax.numpy as jnp
import numpy as np
from jax import lax
from jax.experimental import pallas as pl
from jax.experimental.pallas import tpu as pltpu
from jax.sharding import PartitionSpec as P

RIM = 64
LANES = 128
F32 = jnp.float32
BF16 = jnp.bfloat16
VMEM = pl.BlockSpec(memory_space=pltpu.VMEM)
SMEM = pl.BlockSpec(memory_space=pltpu.SMEM)
HBM = pl.BlockSpec(memory_space=pltpu.MemorySpace.HBM)


def call(body, out_shape, inputs, specs=None, outs=VMEM, scratch=(), flops=0, aliases=None, name=None):
    out_specs = jax.tree.map(lambda _: outs, out_shape)
    moved = sum(x.size * x.dtype.itemsize for x in inputs)
    moved += sum(x.size * x.dtype.itemsize for x in jax.tree.leaves(out_shape))
    return pl.pallas_call(
        body,
        out_shape=out_shape,
        in_specs=specs or [VMEM] * len(inputs),
        out_specs=out_specs,
        scratch_shapes=list(scratch),
        compiler_params=pltpu.CompilerParams(vmem_limit_bytes=24 << 20),
        input_output_aliases=aliases or {},
        cost_estimate=pl.CostEstimate(flops=flops, bytes_accessed=moved, transcendentals=0),
        name=name,
    )(*inputs)


def sds(*shape, dtype=BF16):
    return jax.ShapeDtypeStruct(shape, dtype)


def sincos(x):
    y = x * 0.5
    q = y * y
    sine = 1.0
    for n in (11, 9, 7, 5, 3):
        sine = 1.0 - q * sine * (1.0 / (n * (n - 1)))
    sine = sine * y
    cosine = 1.0
    for n in (12, 10, 8, 6, 4, 2):
        cosine = 1.0 - q * cosine * (1.0 / (n * (n - 1)))
    return 2.0 * sine * cosine, 1.0 - 2.0 * sine * sine


def dft_tables(points):
    products = np.outer(np.arange(points), np.arange(points)) % points
    angles = products * (-2.0 * math.pi / points)
    scale = 1.0 / math.sqrt(points)
    return (np.cos(angles) * scale).astype(np.float32), (np.sin(angles) * scale).astype(np.float32)


def odd_row(columns):
    return lax.rem(lax.axis_index("tile") // columns, 2) == 1


def odd_column():
    return lax.rem(lax.axis_index("tile"), 2) == 1


def rim_body(columns, amp_ref, phase_ref, first_ref, second_ref, held, sem):
    slices, size = amp_ref.shape[0], amp_ref.shape[-1]
    odd = odd_row(columns)
    copies = {}
    for block in range(2):
        top = odd if block == 0 else jnp.logical_not(odd)
        start = pl.multiple_of(jnp.where(top, 0, size - RIM), RIM)
        for s in range(slices):
            for i, ref in enumerate((phase_ref, amp_ref)):
                copy = pltpu.make_async_copy(
                    ref.at[s, pl.ds(start, RIM), :], held.at[block, s, i], sem.at[block, s, i]
                )
                copy.start()
                copies[block, s, i] = copy
    for block, out in enumerate((first_ref, second_ref)):
        for s in range(slices):
            copies[block, s, 0].wait()
            sine, cosine = sincos(held[block, s, 0])
            copies[block, s, 1].wait()
            amp = held[block, s, 1]
            out[s, 0] = (amp * cosine).astype(BF16)
            out[s, 1] = (amp * sine).astype(BF16)


def transmit_body(amp_ref, phase_ref, t_ref, held, sem):
    slices = amp_ref.shape[0]
    copies = []
    for s in range(slices):
        for i, ref in enumerate((phase_ref, amp_ref)):
            copies.append(pltpu.make_async_copy(ref.at[s], held.at[s, i], sem.at[s, i]))
            copies[-1].start()
    for s in range(slices):
        copies[2 * s].wait()
        copies[2 * s + 1].wait()
        sine, cosine = sincos(held[s, 0])
        amp = held[s, 1]
        t_ref[s, 0] = (amp * cosine).astype(BF16)
        t_ref[s, 1] = (amp * sine).astype(BF16)


def lane_halves(low, high):
    lane = lax.broadcasted_iota(jnp.int32, low.shape, 1)
    return jnp.where(lane < RIM, low, high)


def swap(x):
    return pltpu.roll(x, RIM, 1)


def column_body(columns, t_ref, row_first_ref, row_second_ref, first_ref, second_ref):
    size = t_ref.shape[-1]
    flip = odd_row(columns)
    odd = odd_column()
    for s in range(t_ref.shape[0]):
        for start, rows in ((0, RIM), (RIM, size), (RIM + size, RIM)):
            dst = pl.ds(start, rows)

            def load(part, lanes):
                if start == RIM:
                    return t_ref[s, part, :, lanes].astype(F32)
                first = row_first_ref[s, part, :, lanes].astype(F32)
                second = row_second_ref[s, part, :, lanes].astype(F32)
                return jnp.where(flip == (start == 0), first, second)

            low, high = slice(0, LANES), slice(size - LANES, size)
            left = lane_halves(load(0, low), swap(load(1, low)))
            right = lane_halves(swap(load(0, high)), load(1, high))
            first_ref[s, dst, :] = jnp.where(odd, right, left).astype(BF16)
            second_ref[s, dst, :] = jnp.where(odd, left, right).astype(BF16)


def extend_body(columns, t_ref, row_first_ref, row_second_ref, ext_ref):
    slices, size = t_ref.shape[0], t_ref.shape[-1]
    flip = odd_row(columns)
    for s in range(slices):
        for part in range(2):
            for tile in range(size // LANES):
                lanes = slice(tile * LANES, (tile + 1) * LANES)
                first = row_first_ref[s, part, :, lanes].astype(F32)
                second = row_second_ref[s, part, :, lanes].astype(F32)
                ext_ref[tile, s, part, :RIM] = jnp.where(flip, first, second)
                ext_ref[tile, s, part, RIM : RIM + size] = t_ref[s, part, :, lanes].astype(F32)
                ext_ref[tile, s, part, RIM + size :] = jnp.where(flip, second, first)


def lane_place(column, size):
    tiles = (size + 2 * RIM) // LANES
    place = jnp.where(column < 0, column + size + 2 * RIM, column)
    first = place // LANES
    second = jnp.where(first == tiles - 1, 0, first + 1)
    return first, second, place % LANES


def cut_body(count, size, pos_ref, rim_first_ref, rim_second_ref, ext_in, ext, *outs):
    del ext_in
    slices = ext.shape[1]
    odd = odd_column()
    for s in range(slices):
        first = rim_first_ref[s].astype(F32)
        second = rim_second_ref[s].astype(F32)
        left = jnp.where(odd, second, first)
        right = jnp.where(odd, first, second)
        ext[size // LANES, s, 0] = lane_halves(right, swap(left))
        ext[size // LANES, s, 1] = lane_halves(swap(right), left)
    depth = lax.axis_index("depth")
    for k in range(count):
        wave = depth ^ k
        row = pos_ref[wave, 0] + RIM
        first, second, shift = lane_place(pos_ref[wave, 1], size)
        turn = lax.rem(LANES - shift, LANES)
        lane = lax.broadcasted_iota(jnp.int32, (LANES, LANES), 1)
        for s in range(slices):
            for part in range(2):
                low = ext[first, s, part, pl.ds(row, LANES), :]
                high = ext[second, s, part, pl.ds(row, LANES), :]
                mixed = jnp.where(lane >= shift, low, high)
                outs[k][s, part] = pltpu.roll(mixed.astype(BF16), turn, 1)


def operator_body(phase_ref, dft_real_ref, dft_imag_ref, fwd_ref, bwd_ref):
    fr = dft_real_ref[...]
    fi = dft_imag_ref[...]
    n = fr.shape[0]

    def dot(a, b):
        return jnp.dot(a, b, precision=lax.Precision.HIGHEST, preferred_element_type=F32)

    def put(index, real, imag, flip):
        rt, it = real.T, imag.T
        plain = ((real, imag), (-imag, real))
        turned = ((rt, -it), (it, rt))
        for i in range(2):
            for j in range(2):
                rows, cols = pl.ds(i * n, n), pl.ds(j * n, n)
                value = (turned if flip else plain)[i][j]
                high = value.astype(BF16)
                fwd_ref[index, 0, rows, cols] = high
                fwd_ref[index, 1, rows, cols] = (value - high.astype(F32)).astype(BF16)
                bwd_ref[index, rows, cols] = (plain if flip else turned)[i][j].astype(BF16)

    for axis in range(2):
        sine, cosine = sincos(phase_ref[axis : axis + 1, :])
        er = fr * cosine - fi * sine
        ei = fr * sine + fi * cosine
        real = dot(er, fr) + dot(ei, fi)
        imag = dot(ei, fr) - dot(er, fi)
        put(axis, real, imag, axis == 0)
        put(2 + axis, er, ei, axis == 0)


def split(x):
    high = x.astype(BF16)
    return high, (x - high.astype(F32)).astype(BF16)


def mm(a, b):
    return jnp.dot(a, b, preferred_element_type=F32)


def left_fine(fwd_ref, index, real, imag):
    n = real.shape[0]
    high, low = split(jnp.concatenate([real, imag], axis=0))
    both = mm(fwd_ref[index, 0], jnp.concatenate([high, low], axis=1))
    out = both[:, :n] + both[:, n:] + mm(fwd_ref[index, 1], high)
    return out[:n], out[n:]


def right_fine(fwd_ref, index, real, imag):
    n = real.shape[0]
    high, low = split(jnp.concatenate([real, imag], axis=1))
    both = mm(jnp.concatenate([high, low], axis=0), fwd_ref[index, 0])
    out = both[:n] + both[n:] + mm(high, fwd_ref[index, 1])
    return out[:, :n], out[:, n:]


def left_plain(bwd_ref, index, real, imag):
    n = real.shape[0]
    out = mm(bwd_ref[index], jnp.concatenate([real, imag], axis=0).astype(BF16))
    return out[:n], out[n:]


def right_plain(bwd_ref, index, real, imag):
    n = real.shape[0]
    out = mm(jnp.concatenate([real, imag], axis=1).astype(BF16), bwd_ref[index])
    return out[:, :n], out[:, n:]


def wave_body(count, fwd_ref, bwd_ref, probe_ref, measured_ref, *rest):
    windows, outs = rest[:count], rest[count : 2 * count]
    patch, waves, grads = rest[2 * count :]
    depth = lax.axis_index("depth")
    slices = windows[0].shape[0]
    total = slices * count
    for k in range(count):
        patch[depth ^ k] = windows[k][...]

    def patch_of(s):
        group, local = s // slices, s % slices
        return patch[group, local, 0].astype(F32), patch[group, local, 1].astype(F32)

    def mix(s, wr, wi):
        pr, pi = patch_of(s)
        waves[s, 0] = wr
        waves[s, 1] = wi
        return pr * wr - pi * wi, pr * wi + pi * wr

    def forward(s, wave):
        half = left_fine(fwd_ref, 0, *mix(s, *wave))
        return right_fine(fwd_ref, 1, *half)

    wave = lax.fori_loop(0, total - 1, forward, (probe_ref[0], probe_ref[1]), unroll=True)
    half = left_fine(fwd_ref, 2, *mix(total - 1, *wave))
    far_real, far_imag = right_fine(fwd_ref, 3, *half)
    misfit = far_real * far_real + far_imag * far_imag - measured_ref[depth]
    half = left_plain(bwd_ref, 2, misfit * far_real, misfit * far_imag)
    spread = right_plain(bwd_ref, 3, *half)

    def contribute(s, sr, si):
        wr, wi = waves[s, 0], waves[s, 1]
        group, local = s // slices, s % slices
        grads[group, local, 0] = (wr * sr + wi * si).astype(BF16)
        grads[group, local, 1] = (wr * si - wi * sr).astype(BF16)

    def backward(step, spread):
        s = total - 1 - step
        sr, si = spread
        contribute(s, sr, si)
        pr, pi = patch_of(s)
        half = left_plain(bwd_ref, 0, pr * sr + pi * si, pr * si - pi * sr)
        return right_plain(bwd_ref, 1, *half)

    spread = lax.fori_loop(0, total - 1, backward, spread, unroll=True)
    contribute(0, *spread)
    for k in range(count):
        outs[k][...] = grads[depth ^ k]


def deposit_body(count, size, pos_ref, *rest):
    grads = rest[:count]
    ext, first_ref, second_ref = rest[count:]
    tiles = ext.shape[0]
    slices = grads[0].shape[0]
    ext[...] = jnp.zeros_like(ext)
    depth = lax.axis_index("depth")
    odd = odd_column()
    for k in range(count):
        wave = depth ^ k
        row = pos_ref[wave, 0] + RIM
        first, second, shift = lane_place(pos_ref[wave, 1], size)
        lane = lax.broadcasted_iota(jnp.int32, (LANES, LANES), 1)
        rows = pl.ds(row, LANES)
        for s in range(slices):
            for part in range(2):
                moved = pltpu.roll(grads[k][s, part], shift, 1).astype(F32)
                low = jnp.where(lane >= shift, moved, 0.0)
                ext[first, s, part, rows, :] += low
                ext[second, s, part, rows, :] += moved - low
    for s in range(slices):
        real, imag = ext[tiles - 1, s, 0], ext[tiles - 1, s, 1]
        right = lane_halves(real, swap(imag))
        left = lane_halves(swap(real), imag)
        first_ref[s] = jnp.where(odd, right, left).astype(BF16)
        second_ref[s] = jnp.where(odd, left, right).astype(BF16)


def halves_added(odd, ext_ref, rim_first_ref, rim_second_ref, s, part, rows):
    first = rim_first_ref[s, rows, :].astype(F32)
    second = rim_second_ref[s, rows, :].astype(F32)
    left = jnp.where(odd, second, first)
    right = jnp.where(odd, first, second)
    if part == 0:
        right = swap(right)
    else:
        left = swap(left)
    last = ext_ref.shape[0] - 2
    zero = jnp.zeros_like(left)
    return (
        ext_ref[0, s, part, rows, :] + lane_halves(left, zero),
        ext_ref[last, s, part, rows, :] + lane_halves(zero, right),
    )


def row_body(columns, ext_ref, rim_first_ref, rim_second_ref, first_ref, second_ref):
    height = ext_ref.shape[-2]
    odd = odd_column()
    flip = odd_row(columns)
    for s in range(ext_ref.shape[1]):
        for part in range(2):
            refs = (odd, ext_ref, rim_first_ref, rim_second_ref, s, part)
            above = halves_added(*refs, pl.ds(0, RIM))
            below = halves_added(*refs, pl.ds(height - RIM, RIM))
            for tile in range(2):
                lanes = slice(tile * LANES, (tile + 1) * LANES)
                up, down = above[tile], below[tile]
                first_ref[s, part, :, lanes] = jnp.where(flip, up, down).astype(BF16)
                second_ref[s, part, :, lanes] = jnp.where(flip, down, up).astype(BF16)


def put_rows(out_ref, held, sem, blocks):
    copies = []
    for part in range(out_ref.shape[0]):
        for s in range(out_ref.shape[1]):
            at = 0
            for i, (start, rows) in enumerate(blocks):
                copy = pltpu.make_async_copy(
                    held.at[part, s, pl.ds(at, rows), :],
                    out_ref.at[part, s, pl.ds(start, rows), :],
                    sem.at[part, s, i],
                )
                copies.append(copy)
                at += rows
    return copies


def middle_body(ext_ref, rim_first_ref, rim_second_ref, out_ref, held, sem):
    size = out_ref.shape[-1]
    odd = odd_column()
    copies = put_rows(out_ref, held, sem, ((RIM, size - 2 * RIM),))
    for part in range(2):
        for s in range(ext_ref.shape[1]):
            rows = pl.ds(2 * RIM, size - 2 * RIM)
            pieces = halves_added(odd, ext_ref, rim_first_ref, rim_second_ref, s, part, rows)
            for tile, piece in enumerate(pieces):
                held[part, s, :, tile * LANES : (tile + 1) * LANES] = piece
    for copy in copies:
        copy.start()
    for copy in copies:
        copy.wait()


def edge_body(columns, ext_ref, rim_first_ref, rim_second_ref, *rest):
    row_first_ref, row_second_ref, out_in, out_ref, held, sem = rest
    del out_in
    size = out_ref.shape[-1]
    odd = odd_column()
    flip = odd_row(columns)
    blocks = ((0, RIM), (size - RIM, RIM))
    copies = put_rows(out_ref, held, sem, blocks)
    for part in range(2):
        for s in range(ext_ref.shape[1]):
            for i, (start, rows) in enumerate(blocks):
                refs = (odd, ext_ref, rim_first_ref, rim_second_ref, s, part)
                pieces = halves_added(*refs, pl.ds(RIM + start, rows))
                for tile, piece in enumerate(pieces):
                    lanes = slice(tile * LANES, (tile + 1) * LANES)
                    first = row_first_ref[s, part, :, lanes].astype(F32)
                    second = row_second_ref[s, part, :, lanes].astype(F32)
                    piece = piece + jnp.where(flip == (start == 0), first, second)
                    held[part, s, i * RIM : (i + 1) * RIM, lanes] = piece
                copies[(part * ext_ref.shape[1] + s) * 2 + i].start()
    for copy in copies:
        copy.wait()


def shards(amplitude, phase_map, probe_wave, propagator_phase, positions, measured):
    slices, size = amplitude.shape[0], amplitude.shape[-1]
    points = probe_wave.shape[-1]
    count = lax.axis_size("depth")
    tiles = lax.axis_size("tile")
    columns = max(2, tiles // 8)
    pos = positions[0]

    def row_swap(x, odd):
        low = [i for i in range(tiles - columns) if i // columns % 2 == odd]
        pairs = [(i, i + columns) for i in low] + [(i + columns, i) for i in low]
        return lax.ppermute(x, "tile", pairs)

    def column_swap(x, odd):
        low = [i for i in range(tiles) if i % 2 == odd and i % columns + 1 < columns]
        pairs = [(i, i + 1) for i in low] + [(i + 1, i) for i in low]
        return lax.ppermute(x, "tile", pairs)

    def depth_swap(x, by):
        return lax.ppermute(x, "depth", [(i, i ^ by) for i in range(count)])

    rim_rows = sds(slices, 2, RIM, size)
    rim_cols = sds(slices, size + 2 * RIM, LANES)
    window = sds(slices, 2, points, points)
    ext = sds((size + 2 * RIM) // LANES, slices, 2, size + 2 * RIM, LANES, dtype=F32)
    amplitude, phase_map = (
        pltpu.with_memory_space_constraint(x[:, 0], pltpu.MemorySpace.HBM)
        for x in (amplitude, phase_map)
    )
    first, second = call(
        functools.partial(rim_body, columns),
        (rim_rows, rim_rows),
        (amplitude, phase_map),
        specs=[HBM, HBM],
        scratch=(
            pltpu.VMEM((2, slices, 2, RIM, size), F32),
            pltpu.SemaphoreType.DMA((2, slices, 2)),
        ),
        flops=40 * 4 * RIM * size,
        name="row_rims_out",
    )
    rows = row_swap(first, 0), row_swap(second, 1)
    trans = call(
        transmit_body,
        sds(slices, 2, size, size),
        (amplitude, phase_map),
        specs=[HBM, HBM],
        scratch=(pltpu.VMEM((slices, 2, size, size), F32), pltpu.SemaphoreType.DMA((slices, 2))),
        flops=40 * 2 * size * size,
        name="transmit",
    )
    dft_real, dft_imag = dft_tables(points)
    fwd, bwd = call(
        operator_body,
        (sds(4, 2, 2 * points, 2 * points), sds(4, 2 * points, 2 * points)),
        (propagator_phase, jnp.asarray(dft_real), jnp.asarray(dft_imag)),
        flops=8 * 6 * 2 * points**3,
        name="operators",
    )
    first, second = call(
        functools.partial(column_body, columns),
        (rim_cols, rim_cols),
        (trans, *rows),
        name="column_rims_out",
    )
    cols = column_swap(first, 1), column_swap(second, 0)
    extended = call(functools.partial(extend_body, columns), ext, (trans, *rows), name="extend")
    windows = call(
        functools.partial(cut_body, count, size),
        (ext,) + (window,) * count,
        (pos, *cols, extended),
        specs=[SMEM] + [VMEM] * 3,
        aliases={3: 0},
        name="cut",
    )[1:]
    arrived = [windows[0]] + [depth_swap(windows[k], k) for k in range(1, count)]
    total = slices * count
    grads = call(
        functools.partial(wave_body, count),
        (window,) * count,
        (fwd, bwd, probe_wave, measured[0], *arrived),
        scratch=(
            pltpu.VMEM((count, slices, 2, points, points), BF16),
            pltpu.VMEM((total, 2, points, points), F32),
            pltpu.VMEM((count, slices, 2, points, points), BF16),
        ),
        flops=36 * 8 * 2 * points**3,
        name="waves",
    )
    returned = [grads[0]] + [depth_swap(grads[k], k) for k in range(1, count)]
    summed, first, second = call(
        functools.partial(deposit_body, count, size),
        (ext, rim_cols, rim_cols),
        (pos, *returned),
        specs=[SMEM] + [VMEM] * count,
        name="deposit",
    )
    cols = column_swap(first, 1), column_swap(second, 0)
    first, second = call(
        functools.partial(row_body, columns),
        (rim_rows, rim_rows),
        (summed, *cols),
        name="row_rims_back",
    )
    rows = row_swap(first, 0), row_swap(second, 1)
    gradient = sds(2, slices, size, size, dtype=F32)
    middle = call(
        middle_body,
        gradient,
        (summed, *cols),
        outs=HBM,
        scratch=(
            pltpu.VMEM((2, slices, size - 2 * RIM, size), F32),
            pltpu.SemaphoreType.DMA((2, slices, 1)),
        ),
        name="middle_rows",
    )
    gradient = call(
        functools.partial(edge_body, columns),
        gradient,
        (summed, *cols, *rows, middle),
        specs=[VMEM] * 5 + [HBM],
        outs=HBM,
        scratch=(
            pltpu.VMEM((2, slices, 2 * RIM, size), F32),
            pltpu.SemaphoreType.DMA((2, slices, 2)),
        ),
        aliases={5: 0},
        name="edge_rows",
    )
    return gradient[:, :, None]


def solution(mesh):
    in_specs = (
        P("depth", "tile", None, None),
        P("depth", "tile", None, None),
        P(),
        P(),
        P("tile", None, None),
        P("tile", None, None, None),
    )
    out_specs = P(None, "depth", "tile", None, None)
    return jax.shard_map(shards, mesh=mesh, in_specs=in_specs, out_specs=out_specs, check_vma=False)
```

```python
import functools
import math

import jax
import jax.numpy as jnp
import numpy as np
from jax import lax
from jax.experimental import pallas as pl
from jax.experimental.pallas import tpu as pltpu
from jax.sharding import PartitionSpec as P

RIM = 64
LANES = 128
F32 = jnp.float32
BF16 = jnp.bfloat16
VMEM = pl.BlockSpec(memory_space=pltpu.VMEM)
SMEM = pl.BlockSpec(memory_space=pltpu.SMEM)
HBM = pl.BlockSpec(memory_space=pltpu.MemorySpace.HBM)


def call(body, out_shape, inputs, specs=None, outs=VMEM, scratch=(), flops=0, aliases=None, name=None):
    out_specs = jax.tree.map(lambda _: outs, out_shape)
    moved = sum(x.size * x.dtype.itemsize for x in inputs)
    moved += sum(x.size * x.dtype.itemsize for x in jax.tree.leaves(out_shape))
    return pl.pallas_call(
        body,
        out_shape=out_shape,
        in_specs=specs or [VMEM] * len(inputs),
        out_specs=out_specs,
        scratch_shapes=list(scratch),
        compiler_params=pltpu.CompilerParams(vmem_limit_bytes=24 << 20),
        input_output_aliases=aliases or {},
        cost_estimate=pl.CostEstimate(flops=flops, bytes_accessed=moved, transcendentals=0),
        name=name,
    )(*inputs)


def sds(*shape, dtype=BF16):
    return jax.ShapeDtypeStruct(shape, dtype)


def sincos(x):
    y = x * 0.5
    q = y * y
    sine = 1.0
    for n in (11, 9, 7, 5, 3):
        sine = 1.0 - q * sine * (1.0 / (n * (n - 1)))
    sine = sine * y
    cosine = 1.0
    for n in (12, 10, 8, 6, 4, 2):
        cosine = 1.0 - q * cosine * (1.0 / (n * (n - 1)))
    return 2.0 * sine * cosine, 1.0 - 2.0 * sine * sine


def dft_tables(points):
    products = np.outer(np.arange(points), np.arange(points)) % points
    angles = products * (-2.0 * math.pi / points)
    scale = 1.0 / math.sqrt(points)
    return (np.cos(angles) * scale).astype(np.float32), (np.sin(angles) * scale).astype(np.float32)


def odd_row(columns):
    return lax.rem(lax.axis_index("tile") // columns, 2) == 1


def odd_column():
    return lax.rem(lax.axis_index("tile"), 2) == 1


def rim_body(columns, amp_ref, phase_ref, first_ref, second_ref, held, sem):
    slices, size = amp_ref.shape[0], amp_ref.shape[-1]
    odd = odd_row(columns)
    copies = {}
    for block in range(2):
        top = odd if block == 0 else jnp.logical_not(odd)
        start = pl.multiple_of(jnp.where(top, 0, size - RIM), RIM)
        for s in range(slices):
            for i, ref in enumerate((phase_ref, amp_ref)):
                copy = pltpu.make_async_copy(
                    ref.at[s, pl.ds(start, RIM), :], held.at[block, s, i], sem.at[block, s, i]
                )
                copy.start()
                copies[block, s, i] = copy
    for block, out in enumerate((first_ref, second_ref)):
        for s in range(slices):
            copies[block, s, 0].wait()
            sine, cosine = sincos(held[block, s, 0])
            copies[block, s, 1].wait()
            amp = held[block, s, 1]
            out[s, 0] = (amp * cosine).astype(BF16)
            out[s, 1] = (amp * sine).astype(BF16)


def transmit_body(amp_ref, phase_ref, t_ref, held, sem):
    slices = amp_ref.shape[0]
    copies = []
    for s in range(slices):
        for i, ref in enumerate((phase_ref, amp_ref)):
            copies.append(pltpu.make_async_copy(ref.at[s], held.at[s, i], sem.at[s, i]))
            copies[-1].start()
    for s in range(slices):
        copies[2 * s].wait()
        copies[2 * s + 1].wait()
        sine, cosine = sincos(held[s, 0])
        amp = held[s, 1]
        t_ref[s, 0] = (amp * cosine).astype(BF16)
        t_ref[s, 1] = (amp * sine).astype(BF16)


def lane_halves(low, high):
    lane = lax.broadcasted_iota(jnp.int32, low.shape, 1)
    return jnp.where(lane < RIM, low, high)


def swap(x):
    return pltpu.roll(x, RIM, 1)


def column_body(columns, t_ref, row_first_ref, row_second_ref, first_ref, second_ref):
    size = t_ref.shape[-1]
    flip = odd_row(columns)
    odd = odd_column()
    for s in range(t_ref.shape[0]):
        for start, rows in ((0, RIM), (RIM, size), (RIM + size, RIM)):
            dst = pl.ds(start, rows)

            def load(part, lanes):
                if start == RIM:
                    return t_ref[s, part, :, lanes].astype(F32)
                first = row_first_ref[s, part, :, lanes].astype(F32)
                second = row_second_ref[s, part, :, lanes].astype(F32)
                return jnp.where(flip == (start == 0), first, second)

            low, high = slice(0, LANES), slice(size - LANES, size)
            left = lane_halves(load(0, low), swap(load(1, low)))
            right = lane_halves(swap(load(0, high)), load(1, high))
            first_ref[s, dst, :] = jnp.where(odd, right, left).astype(BF16)
            second_ref[s, dst, :] = jnp.where(odd, left, right).astype(BF16)


def extend_body(columns, t_ref, row_first_ref, row_second_ref, ext_ref):
    slices, size = t_ref.shape[0], t_ref.shape[-1]
    flip = odd_row(columns)
    for s in range(slices):
        for part in range(2):
            for tile in range(size // LANES):
                lanes = slice(tile * LANES, (tile + 1) * LANES)
                first = row_first_ref[s, part, :, lanes].astype(F32)
                second = row_second_ref[s, part, :, lanes].astype(F32)
                ext_ref[tile, s, part, :RIM] = jnp.where(flip, first, second)
                ext_ref[tile, s, part, RIM : RIM + size] = t_ref[s, part, :, lanes].astype(F32)
                ext_ref[tile, s, part, RIM + size :] = jnp.where(flip, second, first)


def lane_place(column, size):
    tiles = (size + 2 * RIM) // LANES
    place = jnp.where(column < 0, column + size + 2 * RIM, column)
    first = place // LANES
    second = jnp.where(first == tiles - 1, 0, first + 1)
    return first, second, place % LANES


def cut_body(count, size, pos_ref, rim_first_ref, rim_second_ref, ext_in, ext, *outs):
    del ext_in
    slices = ext.shape[1]
    odd = odd_column()
    for s in range(slices):
        first = rim_first_ref[s].astype(F32)
        second = rim_second_ref[s].astype(F32)
        left = jnp.where(odd, second, first)
        right = jnp.where(odd, first, second)
        ext[size // LANES, s, 0] = lane_halves(right, swap(left))
        ext[size // LANES, s, 1] = lane_halves(swap(right), left)
    depth = lax.axis_index("depth")
    for k in range(count):
        wave = depth ^ k
        row = pos_ref[wave, 0] + RIM
        first, second, shift = lane_place(pos_ref[wave, 1], size)
        turn = lax.rem(LANES - shift, LANES)
        lane = lax.broadcasted_iota(jnp.int32, (LANES, LANES), 1)
        for s in range(slices):
            for part in range(2):
                low = ext[first, s, part, pl.ds(row, LANES), :]
                high = ext[second, s, part, pl.ds(row, LANES), :]
                mixed = jnp.where(lane >= shift, low, high)
                outs[k][s, part] = pltpu.roll(mixed.astype(BF16), turn, 1)


def operator_body(phase_ref, dft_real_ref, dft_imag_ref, fwd_ref, bwd_ref):
    fr = dft_real_ref[...]
    fi = dft_imag_ref[...]
    n = fr.shape[0]

    def dot(a, b):
        return jnp.dot(a, b, precision=lax.Precision.HIGHEST, preferred_element_type=F32)

    def put(index, real, imag, flip):
        rt, it = real.T, imag.T
        plain = ((real, imag), (-imag, real))
        turned = ((rt, -it), (it, rt))
        for i in range(2):
            for j in range(2):
                rows, cols = pl.ds(i * n, n), pl.ds(j * n, n)
                value = (turned if flip else plain)[i][j]
                high = value.astype(BF16)
                fwd_ref[index, 0, rows, cols] = high
                fwd_ref[index, 1, rows, cols] = (value - high.astype(F32)).astype(BF16)
                bwd_ref[index, rows, cols] = (plain if flip else turned)[i][j].astype(BF16)

    for axis in range(2):
        sine, cosine = sincos(phase_ref[axis : axis + 1, :])
        er = fr * cosine - fi * sine
        ei = fr * sine + fi * cosine
        real = dot(er, fr) + dot(ei, fi)
        imag = dot(ei, fr) - dot(er, fi)
        put(axis, real, imag, axis == 0)
        put(2 + axis, er, ei, axis == 0)


def split(x):
    high = x.astype(BF16)
    return high, (x - high.astype(F32)).astype(BF16)


def mm(a, b):
    return jnp.dot(a, b, preferred_element_type=F32)


def left_fine(fwd_ref, index, real, imag):
    n = real.shape[0]
    high, low = split(jnp.concatenate([real, imag], axis=0))
    both = mm(fwd_ref[index, 0], jnp.concatenate([high, low], axis=1))
    out = both[:, :n] + both[:, n:] + mm(fwd_ref[index, 1], high)
    return out[:n], out[n:]


def right_fine(fwd_ref, index, real, imag):
    n = real.shape[0]
    high, low = split(jnp.concatenate([real, imag], axis=1))
    both = mm(jnp.concatenate([high, low], axis=0), fwd_ref[index, 0])
    out = both[:n] + both[n:] + mm(high, fwd_ref[index, 1])
    return out[:, :n], out[:, n:]


def left_plain(bwd_ref, index, real, imag):
    n = real.shape[0]
    out = mm(bwd_ref[index], jnp.concatenate([real, imag], axis=0).astype(BF16))
    return out[:n], out[n:]


def right_plain(bwd_ref, index, real, imag):
    n = real.shape[0]
    out = mm(jnp.concatenate([real, imag], axis=1).astype(BF16), bwd_ref[index])
    return out[:, :n], out[:, n:]


def wave_body(count, fwd_ref, bwd_ref, probe_ref, measured_ref, *rest):
    windows, outs = rest[:count], rest[count : 2 * count]
    patch, waves, grads = rest[2 * count :]
    depth = lax.axis_index("depth")
    slices = windows[0].shape[0]
    total = slices * count
    for k in range(count):
        patch[depth ^ k] = windows[k][...]

    def patch_of(s):
        group, local = s // slices, s % slices
        return patch[group, local, 0].astype(F32), patch[group, local, 1].astype(F32)

    def mix(s, wr, wi):
        pr, pi = patch_of(s)
        waves[s, 0] = wr
        waves[s, 1] = wi
        return pr * wr - pi * wi, pr * wi + pi * wr

    def forward(s, wave):
        half = left_fine(fwd_ref, 0, *mix(s, *wave))
        return right_fine(fwd_ref, 1, *half)

    wave = lax.fori_loop(0, total - 1, forward, (probe_ref[0], probe_ref[1]), unroll=True)
    half = left_fine(fwd_ref, 2, *mix(total - 1, *wave))
    far_real, far_imag = right_fine(fwd_ref, 3, *half)
    misfit = far_real * far_real + far_imag * far_imag - measured_ref[depth]
    half = left_plain(bwd_ref, 2, misfit * far_real, misfit * far_imag)
    spread = right_plain(bwd_ref, 3, *half)

    def contribute(s, sr, si):
        wr, wi = waves[s, 0], waves[s, 1]
        group, local = s // slices, s % slices
        grads[group, local, 0] = (wr * sr + wi * si).astype(BF16)
        grads[group, local, 1] = (wr * si - wi * sr).astype(BF16)

    def backward(step, spread):
        s = total - 1 - step
        sr, si = spread
        contribute(s, sr, si)
        pr, pi = patch_of(s)
        half = left_plain(bwd_ref, 0, pr * sr + pi * si, pr * si - pi * sr)
        return right_plain(bwd_ref, 1, *half)

    spread = lax.fori_loop(0, total - 1, backward, spread, unroll=True)
    contribute(0, *spread)
    for k in range(count):
        outs[k][...] = grads[depth ^ k]


def deposit_body(count, size, pos_ref, *rest):
    grads = rest[:count]
    ext, first_ref, second_ref = rest[count:]
    tiles = ext.shape[0]
    slices = grads[0].shape[0]
    ext[...] = jnp.zeros_like(ext)
    depth = lax.axis_index("depth")
    odd = odd_column()
    for k in range(count):
        wave = depth ^ k
        row = pos_ref[wave, 0] + RIM
        first, second, shift = lane_place(pos_ref[wave, 1], size)
        lane = lax.broadcasted_iota(jnp.int32, (LANES, LANES), 1)
        rows = pl.ds(row, LANES)
        for s in range(slices):
            for part in range(2):
                moved = pltpu.roll(grads[k][s, part], shift, 1).astype(F32)
                low = jnp.where(lane >= shift, moved, 0.0)
                ext[first, s, part, rows, :] += low
                ext[second, s, part, rows, :] += moved - low
    for s in range(slices):
        real, imag = ext[tiles - 1, s, 0], ext[tiles - 1, s, 1]
        right = lane_halves(real, swap(imag))
        left = lane_halves(swap(real), imag)
        first_ref[s] = jnp.where(odd, right, left).astype(BF16)
        second_ref[s] = jnp.where(odd, left, right).astype(BF16)


def halves_added(odd, ext_ref, rim_first_ref, rim_second_ref, s, part, rows):
    first = rim_first_ref[s, rows, :].astype(F32)
    second = rim_second_ref[s, rows, :].astype(F32)
    left = jnp.where(odd, second, first)
    right = jnp.where(odd, first, second)
    if part == 0:
        right = swap(right)
    else:
        left = swap(left)
    last = ext_ref.shape[0] - 2
    zero = jnp.zeros_like(left)
    return (
        ext_ref[0, s, part, rows, :] + lane_halves(left, zero),
        ext_ref[last, s, part, rows, :] + lane_halves(zero, right),
    )


def row_body(columns, ext_ref, rim_first_ref, rim_second_ref, first_ref, second_ref):
    height = ext_ref.shape[-2]
    odd = odd_column()
    flip = odd_row(columns)
    for s in range(ext_ref.shape[1]):
        for part in range(2):
            refs = (odd, ext_ref, rim_first_ref, rim_second_ref, s, part)
            above = halves_added(*refs, pl.ds(0, RIM))
            below = halves_added(*refs, pl.ds(height - RIM, RIM))
            for tile in range(2):
                lanes = slice(tile * LANES, (tile + 1) * LANES)
                up, down = above[tile], below[tile]
                first_ref[s, part, :, lanes] = jnp.where(flip, up, down).astype(BF16)
                second_ref[s, part, :, lanes] = jnp.where(flip, down, up).astype(BF16)


def put_rows(out_ref, held, sem, blocks):
    copies = []
    for part in range(out_ref.shape[0]):
        for s in range(out_ref.shape[1]):
            at = 0
            for i, (start, rows) in enumerate(blocks):
                copy = pltpu.make_async_copy(
                    held.at[part, s, pl.ds(at, rows), :],
                    out_ref.at[part, s, pl.ds(start, rows), :],
                    sem.at[part, s, i],
                )
                copies.append(copy)
                at += rows
    return copies


def middle_body(ext_ref, rim_first_ref, rim_second_ref, out_ref, held, sem):
    size = out_ref.shape[-1]
    odd = odd_column()
    copies = put_rows(out_ref, held, sem, ((RIM, size - 2 * RIM),))
    for part in range(2):
        for s in range(ext_ref.shape[1]):
            rows = pl.ds(2 * RIM, size - 2 * RIM)
            pieces = halves_added(odd, ext_ref, rim_first_ref, rim_second_ref, s, part, rows)
            for tile, piece in enumerate(pieces):
                held[part, s, :, tile * LANES : (tile + 1) * LANES] = piece
    for copy in copies:
        copy.start()
    for copy in copies:
        copy.wait()


def edge_body(columns, which, ext_ref, rim_first_ref, rim_second_ref, row_ref, *rest):
    out_in, out_ref, held, sem = rest
    del out_in
    size = out_ref.shape[-1]
    odd = odd_column()
    top = odd_row(columns) == (which == 0)
    start = pl.multiple_of(jnp.where(top, 0, size - RIM), RIM)
    copies = put_rows(out_ref, held, sem, ((start, RIM),))
    slices = ext_ref.shape[1]
    for part in range(2):
        for s in range(slices):
            refs = (odd, ext_ref, rim_first_ref, rim_second_ref, s, part)
            pieces = halves_added(*refs, pl.ds(start + RIM, RIM))
            for tile, piece in enumerate(pieces):
                lanes = slice(tile * LANES, (tile + 1) * LANES)
                held[part, s, :, lanes] = piece + row_ref[s, part, :, lanes].astype(F32)
            copies[part * slices + s].start()
    for copy in copies:
        copy.wait()


def shards(amplitude, phase_map, probe_wave, propagator_phase, positions, measured):
    slices, size = amplitude.shape[0], amplitude.shape[-1]
    points = probe_wave.shape[-1]
    count = lax.axis_size("depth")
    tiles = lax.axis_size("tile")
    columns = max(2, tiles // 8)
    pos = positions[0]

    def row_swap(x, odd):
        low = [i for i in range(tiles - columns) if i // columns % 2 == odd]
        pairs = [(i, i + columns) for i in low] + [(i + columns, i) for i in low]
        return lax.ppermute(x, "tile", pairs)

    def column_swap(x, odd):
        low = [i for i in range(tiles) if i % 2 == odd and i % columns + 1 < columns]
        pairs = [(i, i + 1) for i in low] + [(i + 1, i) for i in low]
        return lax.ppermute(x, "tile", pairs)

    def depth_swap(x, by):
        return lax.ppermute(x, "depth", [(i, i ^ by) for i in range(count)])

    rim_rows = sds(slices, 2, RIM, size)
    rim_cols = sds(slices, size + 2 * RIM, LANES)
    window = sds(slices, 2, points, points)
    ext = sds((size + 2 * RIM) // LANES, slices, 2, size + 2 * RIM, LANES, dtype=F32)
    amplitude, phase_map = (
        pltpu.with_memory_space_constraint(x[:, 0], pltpu.MemorySpace.HBM)
        for x in (amplitude, phase_map)
    )
    first, second = call(
        functools.partial(rim_body, columns),
        (rim_rows, rim_rows),
        (amplitude, phase_map),
        specs=[HBM, HBM],
        scratch=(
            pltpu.VMEM((2, slices, 2, RIM, size), F32),
            pltpu.SemaphoreType.DMA((2, slices, 2)),
        ),
        flops=40 * 4 * RIM * size,
        name="row_rims_out",
    )
    rows = row_swap(first, 0), row_swap(second, 1)
    trans = call(
        transmit_body,
        sds(slices, 2, size, size),
        (amplitude, phase_map),
        specs=[HBM, HBM],
        scratch=(pltpu.VMEM((slices, 2, size, size), F32), pltpu.SemaphoreType.DMA((slices, 2))),
        flops=40 * 2 * size * size,
        name="transmit",
    )
    dft_real, dft_imag = dft_tables(points)
    fwd, bwd = call(
        operator_body,
        (sds(4, 2, 2 * points, 2 * points), sds(4, 2 * points, 2 * points)),
        (propagator_phase, jnp.asarray(dft_real), jnp.asarray(dft_imag)),
        flops=8 * 6 * 2 * points**3,
        name="operators",
    )
    first, second = call(
        functools.partial(column_body, columns),
        (rim_cols, rim_cols),
        (trans, *rows),
        name="column_rims_out",
    )
    cols = column_swap(first, 1), column_swap(second, 0)
    extended = call(functools.partial(extend_body, columns), ext, (trans, *rows), name="extend")
    windows = call(
        functools.partial(cut_body, count, size),
        (ext,) + (window,) * count,
        (pos, *cols, extended),
        specs=[SMEM] + [VMEM] * 3,
        aliases={3: 0},
        name="cut",
    )[1:]
    arrived = [windows[0]] + [depth_swap(windows[k], k) for k in range(1, count)]
    total = slices * count
    grads = call(
        functools.partial(wave_body, count),
        (window,) * count,
        (fwd, bwd, probe_wave, measured[0], *arrived),
        scratch=(
            pltpu.VMEM((count, slices, 2, points, points), BF16),
            pltpu.VMEM((total, 2, points, points), F32),
            pltpu.VMEM((count, slices, 2, points, points), BF16),
        ),
        flops=36 * 8 * 2 * points**3,
        name="waves",
    )
    returned = [grads[0]] + [depth_swap(grads[k], k) for k in range(1, count)]
    summed, first, second = call(
        functools.partial(deposit_body, count, size),
        (ext, rim_cols, rim_cols),
        (pos, *returned),
        specs=[SMEM] + [VMEM] * count,
        name="deposit",
    )
    cols = column_swap(first, 1), column_swap(second, 0)
    first, second = call(
        functools.partial(row_body, columns),
        (rim_rows, rim_rows),
        (summed, *cols),
        name="row_rims_back",
    )
    rows = row_swap(first, 0), row_swap(second, 1)
    gradient = sds(2, slices, size, size, dtype=F32)
    middle = call(
        middle_body,
        gradient,
        (summed, *cols),
        outs=HBM,
        scratch=(
            pltpu.VMEM((2, slices, size - 2 * RIM, size), F32),
            pltpu.SemaphoreType.DMA((2, slices, 1)),
        ),
        name="middle_rows",
    )
    result = middle
    for which in range(2):
        result = call(
            functools.partial(edge_body, columns, which),
            gradient,
            (summed, *cols, rows[which], result),
            specs=[VMEM] * 4 + [HBM],
            outs=HBM,
            scratch=(
                pltpu.VMEM((2, slices, RIM, size), F32),
                pltpu.SemaphoreType.DMA((2, slices, 1)),
            ),
            aliases={4: 0},
            name=f"edge_rows_{which}",
        )
    return result[:, :, None]


def solution(mesh):
    in_specs = (
        P("depth", "tile", None, None),
        P("depth", "tile", None, None),
        P(),
        P(),
        P("tile", None, None),
        P("tile", None, None, None),
    )
    out_specs = P(None, "depth", "tile", None, None)
    return jax.shard_map(shards, mesh=mesh, in_specs=in_specs, out_specs=out_specs, check_vma=False)
```
